32 devices in a mesh: grp: 8 (over z, y), chan: 4 (over x, core).
Axes of the slice: x: 2, y: 2, z: 4, core: 2. Of those that a mesh axis runs over, the one named last changes fastest.
Arguments:
- grad_out: bfloat16 [64, 8, 16, 128], P('grp', 'chan'), may hold values from -6 to 6
- feat_full: bfloat16 [64, 8, 16, 128], P('grp', 'chan'), may hold values from -6 to 6
- filters_full: bfloat16 [3, 3, 3, 128, 128], replicated, may hold values from -0.109375 to 0.109375
- upsample_weight: bfloat16 [2, 2, 2, 512, 128], replicated, may hold values from -0.1875 to 0.1875
- filters_half: bfloat16 [3, 3, 3, 512, 512], P(None, None, None, None, 'chan'), may hold values from -0.0546875 to 0.0546875
Outputs:
- grad_half: bfloat16 [4, 32, 8, 512], P('chan', 'grp')
- taps_grad: float32 [3, 3, 3, 128, 128], P(None, None, None, 'grp', 'chan')
The draws below stay inside these ranges and needn't reach their ends.
All inputs are finite; a program needn't handle non-finite values.
Results may differ from the reference program's by a relative error of at most 0.0058.
Values may be sent and summed in bfloat16 or wider, within the bound.
No kernel may reach another device: no remote copies, remote signals or barrier semaphores. Data moves between devices by JAX's collectives and lax.ppermute only.
A program may use at most 64 MiB of HBM per device.

```python
import jax
import jax.numpy as jnp
from jax import lax

HALF_CH = 512
FULL_CH = 128
NX = 64
NY = 8
NZ = 16


def steps_of(stream_key, shape, pieces, least, high):
    factor_of, own = 1.0, jax.random.fold_in(stream_key, 6)
    for axis_at, shards_of in pieces:
        heights = jnp.exp(jax.random.uniform(jax.random.fold_in(own, axis_at), (shards_of,), jnp.float32, least / len(pieces), high / len(pieces)))
        factor_of = factor_of * jnp.repeat(heights, shape[axis_at] // shards_of).reshape([-1 if axis == axis_at else 1 for axis in range(len(shape))])
    return factor_of


def normal_values(own_key, dims, deviation, most, pieces=(), kind=jnp.bfloat16):
    drawn = jax.random.normal(own_key, dims, jnp.float32) * deviation
    if len(pieces) > 0:
        drawn = steps_of(own_key, dims, pieces, -0.22, 0.18) * drawn
    return jnp.clip(drawn, min=-most, max=most).astype(kind)


def setup_inputs(seed: int = 0) -> dict:
    streams_of = jax.random.split(jax.random.key(seed), 6)
    grad_out = normal_values(streams_of[0], (NX, NY, NZ, FULL_CH), 1.0, 6.0, ((0, 8), (1, 4)))
    feat_full = normal_values(streams_of[1], (NX, NY, NZ, FULL_CH), 1.0, 6.0, ((0, 8), (1, 4)))
    filters_full = normal_values(streams_of[2], (3, 3, 3, FULL_CH, FULL_CH), (27 * FULL_CH) ** -0.5, 0.109375)
    upsample_weight = normal_values(streams_of[3], (2, 2, 2, HALF_CH, FULL_CH), (8 * FULL_CH) ** -0.5, 0.1875)
    filters_half = normal_values(streams_of[4], (3, 3, 3, HALF_CH, HALF_CH), (27 * HALF_CH) ** -0.5, 0.0546875, ((4, 4),))
    return dict(grad_out=grad_out, feat_full=feat_full, filters_full=filters_full, upsample_weight=upsample_weight, filters_half=filters_half)


def conv_transpose(field, weight):
    extent = field.shape[:3]
    padded = jnp.pad(field, ((1, 1), (1, 1), (1, 1), (0, 0)))
    summed = jnp.zeros(extent + (weight.shape[3],), jnp.float32)
    for p in range(3):
        for q in range(3):
            for r in range(3):
                window = padded[2 - p:2 - p + extent[0], 2 - q:2 - q + extent[1], 2 - r:2 - r + extent[2]]
                summed = summed + jnp.einsum("xyzo,io->xyzi", window, weight[p, q, r], precision=lax.Precision.HIGHEST)
    return summed


def reference(grad_out, feat_full, filters_full, upsample_weight, filters_half):
    upward = grad_out.astype(jnp.float32)
    features = feat_full.astype(jnp.float32)
    extent = grad_out.shape[:3]
    channels = grad_out.shape[3]
    input_grad = conv_transpose(upward, filters_full.astype(jnp.float32)).astype(jnp.bfloat16)
    padded = jnp.pad(features, ((1, 1), (1, 1), (1, 1), (0, 0)))
    tap_list = []
    for p in range(3):
        for q in range(3):
            for r in range(3):
                window = padded[p:p + extent[0], q:q + extent[1], r:r + extent[2]]
                tap_list.append(jnp.einsum("xyzi,xyzo->io", window, upward, precision=lax.Precision.HIGHEST))
    taps_grad = jnp.stack(tap_list).reshape(3, 3, 3, channels, channels)
    halves = input_grad.astype(jnp.float32).reshape(extent[0] // 2, 2, extent[1] // 2, 2, extent[2] // 2, 2, channels)
    coarse = jnp.einsum("iajbkcd,abced->jike", halves, upsample_weight.astype(jnp.float32), precision=lax.Precision.HIGHEST).astype(jnp.bfloat16)
    swapped = jnp.transpose(filters_half.astype(jnp.float32), (1, 0, 2, 3, 4))
    grad_half = conv_transpose(coarse.astype(jnp.float32), swapped).astype(jnp.bfloat16)
    return grad_half, taps_grad
```

```python
import jax
import jax.numpy as jnp
from jax import lax
from jax.experimental import pallas as pl
from jax.experimental.pallas import tpu as pltpu
from jax.sharding import PartitionSpec as P

F32 = jnp.float32
BF16 = jnp.bfloat16
NT = (((1,), (1,)), ((), ()))
NN = (((1,), (0,)), ((), ()))


def dot(a, b, dims):
    return lax.dot_general(a, b, dims, preferred_element_type=F32)


def partner(i, k, n):
    return i ^ k if n & (n - 1) == 0 else (k - i) % n


def swap(value, axis, k):
    n = lax.axis_size(axis)
    return lax.ppermute(value, axis, [(i, partner(i, k, n)) for i in range(n)])


def shift(value, axis, step):
    n = lax.axis_size(axis)
    return lax.ppermute(value, axis, [(i, (i + step) % n) for i in range(n)])


def pair(k, n):
    c = lax.axis_index("chan")
    return jnp.bitwise_xor(c, k) if n & (n - 1) == 0 else lax.rem(k - c + n, n)


def coarse_kernel(n, *refs):
    bricks, (full_ref, up_ref, own_ref, left_ref, right_ref, stage, spread) = refs[:n], refs[n:]
    nx, ny, nz, ch = bricks[0].shape
    rows, half_x, half_z = n * ny, nx // 2, nz // 2
    half_y = rows // 2
    width = own_ref.shape[3]
    spread[:, :, 0] = jnp.zeros((4, half_x, nz, ch), BF16)
    spread[:, :, rows + 1] = jnp.zeros((4, half_x, nz, ch), BF16)
    level = lax.broadcasted_iota(jnp.int32, (nx * ny, half_z, ch), 1)
    for k in range(n):
        stage[...] = bricks[k][...].astype(F32).reshape(nx * ny, nz, ch)
        even = stage[:, pl.ds(0, half_z, stride=2), :]
        odd = stage[:, pl.ds(1, half_z, stride=2), :]
        after = jnp.where(level == half_z - 1, 0.0, pltpu.roll(even, half_z - 1, 1))
        before = jnp.where(level == 0, 0.0, pltpu.roll(odd, 1, 1))
        first = pair(k, n) * ny + 1
        for which, value in enumerate((even, after, odd, before)):
            value = value.reshape(half_x, 2, ny, half_z, ch)
            for b in range(ny):
                packed = jnp.concatenate([value[:, 0, b], value[:, 1, b]], axis=1)
                spread[which, :, first + b] = packed.astype(BF16)
    taps = jnp.concatenate(
        [
            jnp.concatenate([full_ref[p, q, r] for q in range(3) for r in range(3)], axis=1)
            for p in range(3)
        ],
        axis=0,
    )
    grads = []
    for order in ((2, 0, 3), (1, 2, 0)):
        window = jnp.concatenate(
            [
                spread[which, :, 2 - q : 2 - q + rows].reshape(half_x * rows * nz, ch)
                for q in range(3)
                for which in order
            ],
            axis=1,
        )
        product = dot(window, taps, NT).reshape(half_x, rows, 2, half_z, 3 * ch)
        planes = {}
        for u in range(-1, nx + 1):
            terms = [
                product[x // 2, :, x % 2, :, p * ch : (p + 1) * ch]
                for p in range(3)
                for x in (u - p + 1,)
                if 0 <= x < nx
            ]
            total = terms[0]
            for term in terms[1:]:
                total = total + term
            planes[u] = total.reshape(half_y, 2, half_z, ch)
        grads.append(planes)
    nothing = jnp.zeros((half_y * half_z, ch), F32)
    columns = []
    for a in range(2):
        for b in range(2):
            for c in range(2):
                pieces = []
                for i in range(-1, half_x + 1):
                    u = 2 * i + a
                    inside = -1 <= u <= nx
                    pieces.append(
                        grads[c][u][:, b].reshape(half_y * half_z, ch) if inside else nothing
                    )
                columns.append(jnp.concatenate(pieces, axis=0).astype(BF16))
    start = pl.multiple_of(lax.axis_index("chan") * width, width)
    up = jnp.concatenate(
        [
            up_ref[a, b, c, pl.ds(start, width), :]
            for a in range(2)
            for b in range(2)
            for c in range(2)
        ],
        axis=1,
    )
    coarse = dot(jnp.concatenate(columns, axis=1), up, NT)
    coarse = coarse.reshape(half_x + 2, half_y, half_z, width)
    own_ref[...] = coarse
    left_ref[...] = coarse[:2]
    right_ref[...] = coarse[half_x:]


def half_kernel(n, m, own_ref, left_ref, right_ref, half_ref, *refs):
    outs, (padded, result) = refs[:n], refs[n:]
    wide_x, half_y, half_z, width = own_ref.shape
    half_x = wide_x - 2
    inputs = half_ref.shape[3]
    g = lax.axis_index("grp")
    low = jnp.where(g > 0, 1.0, 0.0)
    high = jnp.where(g < m - 1, 1.0, 0.0)
    planes = [own_ref[i] for i in range(wide_x)]
    planes[0] = (planes[0] + left_ref[0]) * low
    planes[1] = planes[1] + left_ref[1] * low
    planes[half_x] = planes[half_x] + right_ref[0] * high
    planes[half_x + 1] = (planes[half_x + 1] + right_ref[1]) * high
    padded[:, 0] = jnp.zeros((3, wide_x, half_z, width), F32)
    padded[:, half_y + 1] = jnp.zeros((3, wide_x, half_z, width), F32)
    level = lax.broadcasted_iota(jnp.int32, (half_y, half_z, width), 1)
    for i in range(wide_x):
        plane = planes[i].astype(BF16).astype(F32)
        padded[0, 1 : half_y + 1, i] = jnp.where(
            level == half_z - 1, 0.0, pltpu.roll(plane, half_z - 1, 1)
        )
        padded[1, 1 : half_y + 1, i] = plane
        padded[2, 1 : half_y + 1, i] = jnp.where(level == 0, 0.0, pltpu.roll(plane, 1, 1))
    cells = half_y * half_x * half_z
    total = None
    for p in range(3):
        windows = [
            padded[r, 2 - q : 2 - q + half_y, 2 - p : 2 - p + half_x]
            .reshape(cells, width)
            .astype(BF16)
            for q in range(3)
            for r in range(3)
        ]
        kernels = [half_ref[p, q, r] for q in range(3) for r in range(3)]
        if width % 128 == 0:
            windows = [jnp.concatenate(windows, axis=1)]
            kernels = [jnp.concatenate(kernels, axis=1)]
        for window, kernel in zip(windows, kernels):
            product = dot(window, kernel, NT)
            total = product if total is None else total + product
    share = half_y // n
    result[...] = total.reshape(n, share, half_x, half_z, inputs)
    for k in range(n):
        outs[k][...] = result[pair(k, n)].astype(outs[k].dtype)


def taps_kernel(n, m, *refs):
    grads, feats, (edge_ref, keep_ref, send_ref, spread, table) = (
        refs[:n],
        refs[n : 2 * n],
        refs[2 * n :],
    )
    nx, ny, nz, ch = grads[0].shape
    rows = n * ny
    part = ch // n
    block = ch // m
    spread[:, 0] = jnp.zeros((nx + 1, nz, ch), BF16)
    spread[:, rows + 1] = jnp.zeros((nx + 1, nz, ch), BF16)
    start = lax.axis_index("chan") * part
    source = lax.broadcasted_iota(jnp.int32, (ch, ch), 0)
    target = lax.broadcasted_iota(jnp.int32, (ch, ch), 1)
    copies = (lax.rem(target, part) + start == source) & (target < 3 * part)
    pick = jnp.where(copies, 1.0, 0.0).astype(BF16)
    bits = m.bit_length() - 1
    owner = source // block
    turned = jnp.zeros_like(owner)
    for bit in range(bits):
        turned = turned + (owner // 2**bit % 2) * 2 ** (bits - 1 - bit)
    order = jnp.where(turned * block + lax.rem(source, block) == target, 1.0, 0.0).astype(BF16)
    keep_edge = jnp.where(lax.axis_index("grp") > 0, 1.0, 0.0)
    flipped = {}
    for k in range(n):
        edge_grad = (edge_ref[k].astype(F32) * keep_edge).astype(BF16)
        edge_feat = (edge_ref[n + k].astype(F32) * keep_edge).astype(BF16)
        cells = jnp.concatenate([edge_grad[None], grads[k][...]], axis=0)
        cells = cells.reshape((nx + 1) * ny * nz, ch)
        chosen = dot(cells, pick, NN)
        level = lax.rem(lax.broadcasted_iota(jnp.int32, chosen.shape, 0), nz)
        lane = lax.broadcasted_iota(jnp.int32, chosen.shape, 1)
        count = chosen.shape[0]
        above = jnp.where(level == nz - 1, 0.0, pltpu.roll(chosen, count - 1, 0))
        below = jnp.where(level == 0, 0.0, pltpu.roll(chosen, 1, 0))
        mixed = jnp.where(lane < part, above, jnp.where(lane < 2 * part, chosen, below))
        mixed = mixed.astype(BF16).reshape(nx + 1, ny, nz, ch)
        first = pair(k, n) * ny + 1
        for b in range(ny):
            spread[:, first + b] = mixed[:, b]
        flipped[k] = jnp.concatenate([edge_feat[None], feats[k][...]], axis=0)
    base = None
    totals = []
    for p in range(3):
        totals.append(None)
    for p in range(3):
        grad_from = 1 if p < 2 else 0
        feat_from = 0 if p == 0 else 1
        total = None
        for k in range(n):
            first = pair(k, n) * ny
            feat = flipped[k][feat_from : feat_from + nx].reshape(nx * ny * nz, ch)
            feat = dot(order, feat, (((0,), (1,)), ((), ()))).astype(BF16)
            window = jnp.concatenate(
                [
                    spread[grad_from : grad_from + nx, pl.ds(first + 2 - q, ny)].reshape(
                        nx * ny * nz, ch
                    )
                    for q in range(3)
                ],
                axis=1,
            )
            product = dot(feat, window, NN)
            total = product if total is None else total + product
        for q in range(3):
            at = (3 * p + q) * ch
            table[:, at : at + ch] = total[:, q * ch : (q + 1) * ch]
    half = ch // 2
    bit = lax.rem(lax.axis_index("grp"), 2)
    keep_ref[...] = table[pl.ds(pl.multiple_of(bit * half, half), half), :]
    send_ref[...] = table[pl.ds(pl.multiple_of((1 - bit) * half, half), half), :].astype(BF16)


def finish_kernel(keep_ref, got_ref, out_ref):
    part = out_ref.shape[4]
    ch = keep_ref.shape[1] // 9
    total = keep_ref[...] + got_ref[...].astype(F32)
    for p in range(3):
        for q in range(3):
            for r in range(3):
                at = (3 * p + q) * ch + r * part
                out_ref[p, q, r] = total[:, at : at + part]


def call(kernel, outs, scratch):
    return pl.pallas_call(kernel, out_shape=outs, scratch_shapes=scratch)


def body(grad_out, feat_full, filters_full, upsample_weight, filters_half):
    n, m = lax.axis_size("chan"), lax.axis_size("grp")
    nx, ny, nz, ch = grad_out.shape
    half_x, half_y, half_z = nx // 2, n * ny // 2, nz // 2
    width = filters_half.shape[4]
    shape = jax.ShapeDtypeStruct
    grads = [grad_out] + [swap(grad_out, "chan", k) for k in range(1, n)]
    feats = [feat_full] + [swap(feat_full, "chan", k) for k in range(1, n)]
    edges = jnp.stack([v[nx - 1] for v in grads] + [v[nx - 1] for v in feats])
    edges = shift(edges, "grp", 1)
    border = shape((2, half_y, half_z, width), F32)
    own, left, right = call(
        lambda *refs: coarse_kernel(n, *refs),
        [shape((half_x + 2, half_y, half_z, width), F32), border, border],
        [
            pltpu.VMEM((nx * ny, nz, ch), F32),
            pltpu.VMEM((4, half_x, n * ny + 2, nz, ch), BF16),
        ],
    )(*grads, filters_full, upsample_weight)
    from_left = shift(right, "grp", 1)
    from_right = shift(left, "grp", -1)
    keep, send = call(
        lambda *refs: taps_kernel(n, m, *refs),
        [shape((ch // 2, 9 * ch), F32), shape((ch // 2, 9 * ch), BF16)],
        [
            pltpu.VMEM((nx + 1, n * ny + 2, nz, ch), BF16),
            pltpu.VMEM((ch, 9 * ch), F32),
        ],
    )(*grads, *feats, edges)
    chunk = (half_y // n, half_x, half_z, filters_half.shape[3])
    chunks = call(
        lambda *refs: half_kernel(n, m, *refs),
        [shape(chunk, F32)] + [shape(chunk, BF16)] * (n - 1),
        [
            pltpu.VMEM((3, half_y + 2, half_x + 2, half_z, width), F32),
            pltpu.VMEM((n,) + chunk, F32),
        ],
    )(own, from_left, from_right, filters_half)
    grad_half = chunks[0]
    for k in range(1, n):
        grad_half = grad_half + swap(chunks[k], "chan", k).astype(F32)
    grad_half = grad_half.astype(BF16)
    got = swap(send, "grp", 1)
    for bit in range(1, m.bit_length() - 1):
        total = keep + got.astype(F32)
        half = total.shape[0] // 2
        upper = lax.rem(lax.div(lax.axis_index("grp"), 2**bit), 2) == 1
        keep = jnp.where(upper, total[half:], total[:half])
        send = jnp.where(upper, total[:half], total[half:]).astype(BF16)
        got = swap(send, "grp", 2**bit)
    taps_grad = call(finish_kernel, shape((3, 3, 3, ch // m, ch // n), F32), [])(keep, got)
    return (grad_half, taps_grad)


def solution(mesh):
    in_specs = (
        P("grp", "chan", None, None),
        P("grp", "chan", None, None),
        P(),
        P(),
        P(None, None, None, None, "chan"),
    )
    out_specs = (P("chan", "grp", None, None), P(None, None, None, "grp", "chan"))
    return jax.shard_map(body, mesh=mesh, in_specs=in_specs, out_specs=out_specs, check_vma=False)
```

```python
import jax
import jax.numpy as jnp
from jax import lax
from jax.experimental import pallas as pl
from jax.experimental.pallas import tpu as pltpu
from jax.sharding import PartitionSpec as P


F32 = jnp.float32
BF16 = jnp.bfloat16
LIMIT = 20 * 2**20
HALO = 3
NT = (((1,), (1,)), ((), ()))
NN = (((1,), (0,)), ((), ()))


def dot(a, b, dims):
    return lax.dot_general(a, b, dims, preferred_element_type=F32)


def swap(value, axis, k):
    n = lax.axis_size(axis)
    return lax.ppermute(value, axis, [(i, i ^ k) for i in range(n)])


def shift(value, axis, step):
    n = lax.axis_size(axis)
    return lax.ppermute(value, axis, [(i, (i + step) % n) for i in range(n)])


def pair(k):
    return jnp.bitwise_xor(lax.axis_index("chan"), k)


def fetch_kernel(*refs):
    count = len(refs) // 2
    arrived = refs[2 * count]
    copies = []
    for k in range(count):
        source, target = refs[k], refs[count + k]
        if source.shape != target.shape:
            width = target.shape[3]
            start = pl.multiple_of(lax.axis_index("chan") * width, width)
            source = source.at[:, :, :, pl.ds(start, width), :]
        copies.append(pltpu.make_async_copy(source, target, arrived.at[k]))
    for copy in copies:
        copy.start()
    for copy in copies:
        copy.wait()


def main_kernel(n, m, *refs):
    bricks, rims, (full_ref, up_ref, half_ref) = (
        refs[:n],
        refs[n : 2 * n],
        refs[2 * n : 2 * n + 3],
    )
    outs, (stage, spread, padded, result, held, arrived) = (
        refs[2 * n + 3 : 3 * n + 3],
        refs[3 * n + 3 :],
    )
    load = pltpu.make_async_copy(half_ref, held, arrived)
    load.start()
    nx, ny, nz, ch = bricks[0].shape
    nx = nx // 2
    halo = rims[0].shape[0] // 2
    rows, half_x, half_z = n * ny, nx // 2, nz // 2
    deep = nx + 2 * halo
    pairs = deep // 2
    half_y = rows // 2
    width = up_ref.shape[3]
    spread[:, :, 0] = jnp.zeros((4, pairs, nz, ch), BF16)
    spread[:, :, rows + 1] = jnp.zeros((4, pairs, nz, ch), BF16)
    level = lax.broadcasted_iota(jnp.int32, (deep * ny, half_z, ch), 1)
    for k in range(n):
        stage[: halo * ny] = rims[k][:halo].astype(F32).reshape(halo * ny, nz, ch)
        stage[halo * ny : (halo + nx) * ny] = bricks[k][:nx].astype(F32).reshape(nx * ny, nz, ch)
        stage[(halo + nx) * ny :] = rims[k][halo:].astype(F32).reshape(halo * ny, nz, ch)
        even = stage[:, pl.ds(0, half_z, stride=2), :]
        odd = stage[:, pl.ds(1, half_z, stride=2), :]
        after = jnp.where(level == half_z - 1, 0.0, pltpu.roll(even, half_z - 1, 1))
        before = jnp.where(level == 0, 0.0, pltpu.roll(odd, 1, 1))
        first = pair(k) * ny + 1
        for which, value in enumerate((even, after, odd, before)):
            value = value.reshape(pairs, 2, ny, half_z, ch)
            for b in range(ny):
                packed = jnp.concatenate([value[:, 0, b], value[:, 1, b]], axis=1)
                spread[which, :, first + b] = packed.astype(BF16)
    taps = jnp.concatenate(
        [
            jnp.concatenate([full_ref[p, q, r] for q in range(3) for r in range(3)], axis=1)
            for p in range(3)
        ],
        axis=0,
    )
    grads = []
    for order in ((2, 0, 3), (1, 2, 0)):
        window = jnp.concatenate(
            [
                spread[which, :, 2 - q : 2 - q + rows].reshape(pairs * rows * nz, ch)
                for q in range(3)
                for which in order
            ],
            axis=1,
        )
        product = dot(window, taps, NT).reshape(pairs, rows, 2, half_z, 3 * ch)
        planes = {}
        for u in range(-2, nx + 2):
            total = None
            for p in range(3):
                x = u - p + 1 + halo
                term = product[x // 2, :, x % 2, :, p * ch : (p + 1) * ch]
                total = term if total is None else total + term
            planes[u] = total.reshape(half_y, 2, half_z, ch)
        grads.append(planes)
    columns = []
    for a in range(2):
        for b in range(2):
            for c in range(2):
                pieces = [
                    grads[c][2 * i + a][:, b].reshape(half_y * half_z, ch)
                    for i in range(-1, half_x + 1)
                ]
                columns.append(jnp.concatenate(pieces, axis=0).astype(BF16))
    up = jnp.concatenate(
        [up_ref[a, b, c] for a in range(2) for b in range(2) for c in range(2)], axis=1
    )
    wide_x = half_x + 2
    coarse = dot(jnp.concatenate(columns, axis=1), up, NT).reshape(wide_x, half_y, half_z, width)
    g = lax.axis_index("grp")
    low = jnp.where(g > 0, 1.0, 0.0)
    high = jnp.where(g < m - 1, 1.0, 0.0)
    padded[:, 0] = jnp.zeros((3, wide_x, half_z, width), F32)
    padded[:, half_y + 1] = jnp.zeros((3, wide_x, half_z, width), F32)
    level = lax.broadcasted_iota(jnp.int32, (half_y, half_z, width), 1)
    for i in range(wide_x):
        plane = coarse[i]
        if i == 0:
            plane = plane * low
        if i == wide_x - 1:
            plane = plane * high
        plane = plane.astype(BF16).astype(F32)
        padded[0, 1 : half_y + 1, i] = jnp.where(
            level == half_z - 1, 0.0, pltpu.roll(plane, half_z - 1, 1)
        )
        padded[1, 1 : half_y + 1, i] = plane
        padded[2, 1 : half_y + 1, i] = jnp.where(level == 0, 0.0, pltpu.roll(plane, 1, 1))
    cells = half_y * half_x * half_z
    total = None
    load.wait()
    for p in range(3):
        windows = [
            padded[r, 2 - q : 2 - q + half_y, 2 - p : 2 - p + half_x]
            .reshape(cells, width)
            .astype(BF16)
            for q in range(3)
            for r in range(3)
        ]
        kernels = [held[p, q, r] for q in range(3) for r in range(3)]
        if width % 128 == 0:
            windows = [jnp.concatenate(windows, axis=1)]
            kernels = [jnp.concatenate(kernels, axis=1)]
        for window, kernel in zip(windows, kernels):
            product = dot(window, kernel, NT)
            total = product if total is None else total + product
    result[...] = total.reshape(result.shape)
    for k in range(n):
        outs[k][...] = result[pair(k)].astype(outs[k].dtype)


def taps_kernel(n, m, *refs):
    bricks, rims, (keep_ref, send_ref, spread, table) = (
        refs[:n],
        refs[n : 2 * n],
        refs[2 * n :],
    )
    nx, ny, nz, ch = bricks[0].shape
    nx = nx // 2
    halo = rims[0].shape[0] // 2
    rows = n * ny
    part = ch // n
    block = ch // m
    spread[:, 0] = jnp.zeros((nx + 2, nz, ch), BF16)
    spread[:, rows + 1] = jnp.zeros((nx + 2, nz, ch), BF16)
    start = lax.axis_index("chan") * part
    source = lax.broadcasted_iota(jnp.int32, (ch, ch), 0)
    target = lax.broadcasted_iota(jnp.int32, (ch, ch), 1)
    copies = (lax.rem(target, part) + start == source) & (target < 3 * part)
    pick = jnp.where(copies, 1.0, 0.0).astype(BF16)
    bits = m.bit_length() - 1
    owner = target // block
    turned = jnp.zeros_like(owner)
    for bit in range(bits):
        turned = turned + (owner // 2**bit % 2) * 2 ** (bits - 1 - bit)
    order = jnp.where(turned * block + lax.rem(target, block) == source, 1.0, 0.0).astype(BF16)
    turned_feats = []
    for k in range(n):
        cells = jnp.concatenate(
            [rims[k][halo - 1 : halo], bricks[k][:nx], rims[k][halo : halo + 1]], axis=0
        )
        cells = cells.reshape((nx + 2) * ny * nz, ch)
        chosen = dot(cells, pick, NN)
        level = lax.rem(lax.broadcasted_iota(jnp.int32, chosen.shape, 0), nz)
        lane = lax.broadcasted_iota(jnp.int32, chosen.shape, 1)
        count = chosen.shape[0]
        above = jnp.where(level == nz - 1, 0.0, pltpu.roll(chosen, count - 1, 0))
        below = jnp.where(level == 0, 0.0, pltpu.roll(chosen, 1, 0))
        mixed = jnp.where(lane < part, above, jnp.where(lane < 2 * part, chosen, below))
        mixed = mixed.astype(BF16).reshape(nx + 2, ny, nz, ch)
        first = pair(k) * ny + 1
        for b in range(ny):
            spread[:, first + b] = mixed[:, b]
        feat = bricks[k][nx:].reshape(nx * ny * nz, ch)
        turned_feats.append(dot(order, feat, NT).astype(BF16))
    for p in range(3):
        total = None
        for k in range(n):
            first = pair(k) * ny
            window = jnp.concatenate(
                [
                    spread[2 - p : 2 - p + nx, pl.ds(first + 2 - q, ny)].reshape(
                        nx * ny * nz, ch
                    )
                    for q in range(3)
                ],
                axis=1,
            )
            product = dot(turned_feats[k], window, NN)
            total = product if total is None else total + product
        table[:, 3 * p * ch : (3 * p + 3) * ch] = total
    half = ch // 2
    bit = lax.rem(lax.axis_index("grp"), 2)
    keep_ref[...] = table[pl.ds(pl.multiple_of(bit * half, half), half), :]
    send_ref[...] = table[pl.ds(pl.multiple_of((1 - bit) * half, half), half), :].astype(BF16)


def load_kernel(grad_ref, feat_ref, own_ref, first_ref, last_ref, arrived):
    nx = grad_ref.shape[0]
    halo = first_ref.shape[0]
    copies = [
        pltpu.make_async_copy(grad_ref.at[pl.ds(nx - halo, halo)], last_ref, arrived.at[0]),
        pltpu.make_async_copy(grad_ref.at[pl.ds(0, halo)], first_ref, arrived.at[1]),
        pltpu.make_async_copy(grad_ref, own_ref.at[pl.ds(0, nx)], arrived.at[2]),
        pltpu.make_async_copy(feat_ref, own_ref.at[pl.ds(nx, nx)], arrived.at[3]),
    ]
    for copy in copies:
        copy.start()
    for copy in copies:
        copy.wait()


def rims_kernel(m, left_ref, right_ref, out_ref):
    g = lax.axis_index("grp")
    halo = left_ref.shape[0]
    left = left_ref[...]
    right = right_ref[...]
    out_ref[:halo] = jnp.where(g > 0, left, jnp.zeros_like(left))
    out_ref[halo:] = jnp.where(g < m - 1, right, jnp.zeros_like(right))


def fold_kernel(bit, keep_ref, got_ref, held_ref, send_ref):
    total = keep_ref[...] + got_ref[...].astype(F32)
    half = held_ref.shape[0]
    upper = lax.rem(lax.axis_index("grp") // 2**bit, 2) == 1
    held_ref[...] = jnp.where(upper, total[half:], total[:half])
    send_ref[...] = jnp.where(upper, total[:half], total[half:]).astype(BF16)


def finish_kernel(keep_ref, got_ref, out_ref):
    part = out_ref.shape[4]
    ch = keep_ref.shape[1] // 9
    total = keep_ref[...] + got_ref[...].astype(F32)
    for p in range(3):
        for q in range(3):
            for r in range(3):
                at = (3 * p + q) * ch + r * part
                out_ref[p, q, r] = total[:, at : at + part]


def sum_kernel(*refs):
    inputs, out_ref = refs[:-1], refs[-1]
    total = inputs[0][...]
    for ref in inputs[1:]:
        total = total + ref[...].astype(F32)
    out_ref[...] = total.astype(BF16)


def call(kernel, outs, scratch, inputs, placed=True, far=0):
    spaces = [pltpu.VMEM] * (len(inputs) - far) + [pltpu.HBM] * far
    return pl.pallas_call(
        kernel,
        out_shape=[pltpu.VMEM(v.shape, v.dtype) if placed else v for v in outs],
        in_specs=[pl.BlockSpec(memory_space=space) for space in spaces],
        out_specs=[pl.BlockSpec(memory_space=pltpu.VMEM)] * len(outs),
        scratch_shapes=scratch,
        compiler_params=pltpu.CompilerParams(vmem_limit_bytes=LIMIT),
    )(*[pltpu.with_memory_space_constraint(v, space) for v, space in zip(inputs, spaces)])


def fetch(weights, shapes):
    count = len(weights)
    return pl.pallas_call(
        fetch_kernel,
        out_shape=[pltpu.VMEM(shape, BF16) for shape in shapes],
        in_specs=[pl.BlockSpec(memory_space=pltpu.HBM)] * count,
        out_specs=[pl.BlockSpec(memory_space=pltpu.VMEM)] * count,
        scratch_shapes=[pltpu.SemaphoreType.DMA((count,))],
        compiler_params=pltpu.CompilerParams(vmem_limit_bytes=LIMIT),
    )(*[pltpu.with_memory_space_constraint(v, pltpu.HBM) for v in weights])


def gather(value):
    held = {0: value}
    k = lax.axis_size("chan") // 2
    while k:
        for j in list(held):
            held[j ^ k] = swap(held[j], "chan", k)
        k //= 2
    return [held[j] for j in sorted(held)]


def work(grad_out, feat_full, filters_full, upsample_weight, filters_half):
    n, m = lax.axis_size("chan"), lax.axis_size("grp")
    nx, ny, nz, ch = grad_out.shape
    half_x, half_y, half_z = nx // 2, n * ny // 2, nz // 2
    width = filters_half.shape[4]
    shape = jax.ShapeDtypeStruct
    edge = shape((HALO, ny, nz, ch), BF16)
    own, first, last = call(
        load_kernel,
        [shape((2 * nx, ny, nz, ch), BF16), edge, edge],
        [pltpu.SemaphoreType.DMA((4,))],
        (grad_out, feat_full),
        far=2,
    )
    from_left = shift(last, "grp", 1)
    from_right = shift(first, "grp", -1)
    bricks = gather(own)
    (rim,) = call(
        lambda *refs: rims_kernel(m, *refs),
        [shape((2 * HALO, ny, nz, ch), BF16)],
        [],
        (from_left, from_right),
    )
    rims = gather(rim)
    up = upsample_weight.shape[:3] + (width, ch)
    full, up = fetch((filters_full, upsample_weight), (filters_full.shape, up))
    keep, send = call(
        lambda *refs: taps_kernel(n, m, *refs),
        [shape((ch // 2, 9 * ch), F32), shape((ch // 2, 9 * ch), BF16)],
        [
            pltpu.VMEM((nx + 2, n * ny + 2, nz, ch), BF16),
            pltpu.VMEM((ch, 9 * ch), F32),
        ],
        (*bricks, *rims),
    )
    got = swap(send, "grp", 1)
    chunk = (half_y // n, half_x, half_z, filters_half.shape[3])
    deep = nx + 2 * HALO
    chunks = call(
        lambda *refs: main_kernel(n, m, *refs),
        [shape(chunk, F32)] + [shape(chunk, BF16)] * (n - 1),
        [
            pltpu.VMEM((deep * ny, nz, ch), F32),
            pltpu.VMEM((4, deep // 2, n * ny + 2, nz, ch), BF16),
            pltpu.VMEM((3, half_y + 2, half_x + 2, half_z, width), F32),
            pltpu.VMEM((n,) + chunk, F32),
            pltpu.VMEM(filters_half.shape, BF16),
            pltpu.SemaphoreType.DMA,
        ],
        (*bricks, *rims, full, up, filters_half),
        far=1,
    )
    parts = [chunks[0]]
    for k in range(1, n):
        parts.append(swap(chunks[k], "chan", k))
    (grad_half,) = call(sum_kernel, [shape(chunk, BF16)], [], parts, False)
    for bit in range(1, m.bit_length() - 1):
        rows = keep.shape[0] // 2
        keep, send = call(
            lambda *refs: fold_kernel(bit, *refs),
            [shape((rows, 9 * ch), F32), shape((rows, 9 * ch), BF16)],
            [],
            (keep, got),
        )
        got = swap(send, "grp", 2**bit)
    (taps_grad,) = call(
        finish_kernel, [shape((3, 3, 3, ch // m, ch // n), F32)], [], (keep, got), False
    )
    return (grad_half, taps_grad)


def solution(mesh):
    in_specs = (
        P("grp", "chan", None, None),
        P("grp", "chan", None, None),
        P(),
        P(),
        P(None, None, None, None, "chan"),
    )
    out_specs = (P("chan", "grp", None, None), P(None, None, None, "grp", "chan"))
    return jax.shard_map(work, mesh=mesh, in_specs=in_specs, out_specs=out_specs, check_vma=False)
```

```python
import jax
import jax.numpy as jnp
from jax import lax
from jax.experimental import pallas as pl
from jax.experimental.pallas import tpu as pltpu
from jax.sharding import PartitionSpec as P


F32 = jnp.float32
BF16 = jnp.bfloat16
LIMIT = 20 * 2**20
HALO = 3
NT = (((1,), (1,)), ((), ()))
NN = (((1,), (0,)), ((), ()))


def dot(a, b, dims):
    return lax.dot_general(a, b, dims, preferred_element_type=F32)


def swap(value, axis, k):
    n = lax.axis_size(axis)
    return lax.ppermute(value, axis, [(i, i ^ k) for i in range(n)])


def shift(value, axis, step):
    n = lax.axis_size(axis)
    return lax.ppermute(value, axis, [(i, (i + step) % n) for i in range(n)])


def pair(k):
    return jnp.bitwise_xor(lax.axis_index("chan"), k)


def fetch_kernel(*refs):
    count = len(refs) // 2
    arrived = refs[2 * count]
    copies = []
    for k in range(count):
        source, target = refs[k], refs[count + k]
        if source.shape != target.shape:
            width = target.shape[3]
            start = pl.multiple_of(lax.axis_index("chan") * width, width)
            source = source.at[:, :, :, pl.ds(start, width), :]
        copies.append(pltpu.make_async_copy(source, target, arrived.at[k]))
    for copy in copies:
        copy.start()
    for copy in copies:
        copy.wait()


def main_kernel(n, m, *refs):
    bricks, rims, (full_ref, up_ref, half_ref) = (
        refs[:n],
        refs[n : 2 * n],
        refs[2 * n : 2 * n + 3],
    )
    outs, (stage, spread, padded, result, held, arrived) = (
        refs[2 * n + 3 : 3 * n + 3],
        refs[3 * n + 3 :],
    )
    load = pltpu.make_async_copy(half_ref, held, arrived)
    load.start()
    nx, ny, nz, ch = bricks[0].shape
    nx = nx // 2
    halo = rims[0].shape[0] // 2
    rows, half_x, half_z = n * ny, nx // 2, nz // 2
    deep = nx + 2 * halo
    pairs = deep // 2
    half_y = rows // 2
    width = up_ref.shape[3]
    spread[:, :, 0] = jnp.zeros((4, pairs, nz, ch), BF16)
    spread[:, :, rows + 1] = jnp.zeros((4, pairs, nz, ch), BF16)
    level = lax.broadcasted_iota(jnp.int32, (deep * ny, half_z, ch), 1)
    for k in range(n):
        stage[: halo * ny] = rims[k][:halo].astype(F32).reshape(halo * ny, nz, ch)
        stage[halo * ny : (halo + nx) * ny] = bricks[k][:nx].astype(F32).reshape(nx * ny, nz, ch)
        stage[(halo + nx) * ny :] = rims[k][halo:].astype(F32).reshape(halo * ny, nz, ch)
        even = stage[:, pl.ds(0, half_z, stride=2), :]
        odd = stage[:, pl.ds(1, half_z, stride=2), :]
        after = jnp.where(level == half_z - 1, 0.0, pltpu.roll(even, half_z - 1, 1))
        before = jnp.where(level == 0, 0.0, pltpu.roll(odd, 1, 1))
        first = pair(k) * ny + 1
        for which, value in enumerate((even, after, odd, before)):
            value = value.reshape(pairs, 2, ny, half_z, ch)
            for b in range(ny):
                packed = jnp.concatenate([value[:, 0, b], value[:, 1, b]], axis=1)
                spread[which, :, first + b] = packed.astype(BF16)
    taps = jnp.concatenate(
        [
            jnp.concatenate([full_ref[p, q, r] for q in range(3) for r in range(3)], axis=1)
            for p in range(3)
        ],
        axis=0,
    )
    grads = []
    for order in ((2, 0, 3), (1, 2, 0)):
        window = jnp.concatenate(
            [
                spread[which, :, 2 - q : 2 - q + rows].reshape(pairs * rows * nz, ch)
                for q in range(3)
                for which in order
            ],
            axis=1,
        )
        product = dot(window, taps, NT).reshape(pairs, rows, 2, half_z, 3 * ch)
        planes = {}
        for u in range(-2, nx + 2):
            total = None
            for p in range(3):
                x = u - p + 1 + halo
                term = product[x // 2, :, x % 2, :, p * ch : (p + 1) * ch]
                total = term if total is None else total + term
            planes[u] = total.reshape(half_y, 2, half_z, ch)
        grads.append(planes)
    columns = []
    for a in range(2):
        for b in range(2):
            for c in range(2):
                pieces = [
                    grads[c][2 * i + a][:, b].reshape(half_y * half_z, ch)
                    for i in range(-1, half_x + 1)
                ]
                columns.append(jnp.concatenate(pieces, axis=0).astype(BF16))
    up = jnp.concatenate(
        [up_ref[a, b, c] for a in range(2) for b in range(2) for c in range(2)], axis=1
    )
    wide_x = half_x + 2
    coarse = dot(jnp.concatenate(columns, axis=1), up, NT).reshape(wide_x, half_y, half_z, width)
    g = lax.axis_index("grp")
    low = jnp.where(g > 0, 1.0, 0.0)
    high = jnp.where(g < m - 1, 1.0, 0.0)
    padded[:, 0] = jnp.zeros((3, wide_x, half_z, width), F32)
    padded[:, half_y + 1] = jnp.zeros((3, wide_x, half_z, width), F32)
    level = lax.broadcasted_iota(jnp.int32, (half_y, half_z, width), 1)
    for i in range(wide_x):
        plane = coarse[i]
        if i == 0:
            plane = plane * low
        if i == wide_x - 1:
            plane = plane * high
        plane = plane.astype(BF16).astype(F32)
        padded[0, 1 : half_y + 1, i] = jnp.where(
            level == half_z - 1, 0.0, pltpu.roll(plane, half_z - 1, 1)
        )
        padded[1, 1 : half_y + 1, i] = plane
        padded[2, 1 : half_y + 1, i] = jnp.where(level == 0, 0.0, pltpu.roll(plane, 1, 1))
    cells = half_y * half_x * half_z
    total = None
    load.wait()
    for p in range(3):
        windows = [
            padded[r, 2 - q : 2 - q + half_y, 2 - p : 2 - p + half_x]
            .reshape(cells, width)
            .astype(BF16)
            for q in range(3)
            for r in range(3)
        ]
        kernels = [held[p, q, r] for q in range(3) for r in range(3)]
        if width % 128 == 0:
            windows = [jnp.concatenate(windows, axis=1)]
            kernels = [jnp.concatenate(kernels, axis=1)]
        for window, kernel in zip(windows, kernels):
            product = dot(window, kernel, NT)
            total = product if total is None else total + product
    result[...] = total.reshape(result.shape)
    for k in range(n):
        outs[k][...] = result[pair(k)].astype(outs[k].dtype)


def taps_kernel(n, m, *refs):
    bricks, rims, (keep_ref, send_ref, spread, table) = (
        refs[:n],
        refs[n : 2 * n],
        refs[2 * n :],
    )
    nx, ny, nz, ch = bricks[0].shape
    nx = nx // 2
    halo = rims[0].shape[0] // 2
    rows = n * ny
    part = ch // n
    block = ch // m
    spread[:, 0] = jnp.zeros((nx + 2, nz, ch), BF16)
    spread[:, rows + 1] = jnp.zeros((nx + 2, nz, ch), BF16)
    start = lax.axis_index("chan") * part
    source = lax.broadcasted_iota(jnp.int32, (ch, ch), 0)
    target = lax.broadcasted_iota(jnp.int32, (ch, ch), 1)
    copies = (lax.rem(target, part) + start == source) & (target < 3 * part)
    pick = jnp.where(copies, 1.0, 0.0).astype(BF16)
    bits = m.bit_length() - 1
    owner = target // block
    turned = jnp.zeros_like(owner)
    for bit in range(bits):
        turned = turned + (owner // 2**bit % 2) * 2 ** (bits - 1 - bit)
    order = jnp.where(turned * block + lax.rem(target, block) == source, 1.0, 0.0).astype(BF16)
    turned_feats = []
    for k in range(n):
        cells = jnp.concatenate(
            [rims[k][halo - 1 : halo], bricks[k][:nx], rims[k][halo : halo + 1]], axis=0
        )
        cells = cells.reshape((nx + 2) * ny * nz, ch)
        chosen = dot(cells, pick, NN)
        level = lax.rem(lax.broadcasted_iota(jnp.int32, chosen.shape, 0), nz)
        lane = lax.broadcasted_iota(jnp.int32, chosen.shape, 1)
        count = chosen.shape[0]
        above = jnp.where(level == nz - 1, 0.0, pltpu.roll(chosen, count - 1, 0))
        below = jnp.where(level == 0, 0.0, pltpu.roll(chosen, 1, 0))
        mixed = jnp.where(lane < part, above, jnp.where(lane < 2 * part, chosen, below))
        mixed = mixed.astype(BF16).reshape(nx + 2, ny, nz, ch)
        first = pair(k) * ny + 1
        for b in range(ny):
            spread[:, first + b] = mixed[:, b]
        feat = bricks[k][nx:].reshape(nx * ny * nz, ch)
        turned_feats.append(dot(order, feat, NT).astype(BF16))
    totals = []
    for p in range(3):
        total = None
        for k in range(n):
            first = pair(k) * ny
            window = jnp.concatenate(
                [
                    spread[2 - p : 2 - p + nx, pl.ds(first + 2 - q, ny)].reshape(
                        nx * ny * nz, ch
                    )
                    for q in range(3)
                ],
                axis=1,
            )
            product = dot(turned_feats[k], window, NN)
            total = product if total is None else total + product
        totals += [total[:, q * ch : q * ch + 3 * part] for q in range(3)]
    table[...] = jnp.concatenate(totals, axis=1)
    half = ch // 2
    bit = lax.rem(lax.axis_index("grp"), 2)
    keep_ref[...] = table[pl.ds(pl.multiple_of(bit * half, half), half), :]
    send_ref[...] = table[pl.ds(pl.multiple_of((1 - bit) * half, half), half), :].astype(BF16)


def load_kernel(grad_ref, feat_ref, own_ref, first_ref, last_ref, arrived):
    nx = grad_ref.shape[0]
    halo = first_ref.shape[0]
    copies = [
        pltpu.make_async_copy(grad_ref.at[pl.ds(nx - halo, halo)], last_ref, arrived.at[0]),
        pltpu.make_async_copy(grad_ref.at[pl.ds(0, halo)], first_ref, arrived.at[1]),
        pltpu.make_async_copy(grad_ref, own_ref.at[pl.ds(0, nx)], arrived.at[2]),
        pltpu.make_async_copy(feat_ref, own_ref.at[pl.ds(nx, nx)], arrived.at[3]),
    ]
    for copy in copies:
        copy.start()
    for copy in copies:
        copy.wait()


def rims_kernel(m, left_ref, right_ref, out_ref):
    g = lax.axis_index("grp")
    halo = left_ref.shape[0]
    left = left_ref[...]
    right = right_ref[...]
    out_ref[:halo] = jnp.where(g > 0, left, jnp.zeros_like(left))
    out_ref[halo:] = jnp.where(g < m - 1, right, jnp.zeros_like(right))


def fold_kernel(bit, keep_ref, got_ref, held_ref, send_ref):
    total = keep_ref[...] + got_ref[...].astype(F32)
    half = held_ref.shape[0]
    upper = lax.rem(lax.axis_index("grp") // 2**bit, 2) == 1
    held_ref[...] = jnp.where(upper, total[half:], total[:half])
    send_ref[...] = jnp.where(upper, total[:half], total[half:]).astype(BF16)


def finish_kernel(keep_ref, got_ref, out_ref):
    part = out_ref.shape[4]
    total = keep_ref[...] + got_ref[...].astype(F32)
    for p in range(3):
        for q in range(3):
            for r in range(3):
                at = (9 * p + 3 * q + r) * part
                out_ref[p, q, r] = total[:, at : at + part]


def sum_kernel(*refs):
    inputs, out_ref = refs[:-1], refs[-1]
    total = inputs[0][...]
    for ref in inputs[1:]:
        total = total + ref[...].astype(F32)
    out_ref[...] = total.astype(BF16)


def call(kernel, outs, scratch, inputs, placed=True, far=0):
    spaces = [pltpu.VMEM] * (len(inputs) - far) + [pltpu.HBM] * far
    return pl.pallas_call(
        kernel,
        out_shape=[pltpu.VMEM(v.shape, v.dtype) if placed else v for v in outs],
        in_specs=[pl.BlockSpec(memory_space=space) for space in spaces],
        out_specs=[pl.BlockSpec(memory_space=pltpu.VMEM)] * len(outs),
        scratch_shapes=scratch,
        compiler_params=pltpu.CompilerParams(vmem_limit_bytes=LIMIT),
    )(*[pltpu.with_memory_space_constraint(v, space) for v, space in zip(inputs, spaces)])


def fetch(weights, shapes):
    count = len(weights)
    return pl.pallas_call(
        fetch_kernel,
        out_shape=[pltpu.VMEM(shape, BF16) for shape in shapes],
        in_specs=[pl.BlockSpec(memory_space=pltpu.HBM)] * count,
        out_specs=[pl.BlockSpec(memory_space=pltpu.VMEM)] * count,
        scratch_shapes=[pltpu.SemaphoreType.DMA((count,))],
        compiler_params=pltpu.CompilerParams(vmem_limit_bytes=LIMIT),
    )(*[pltpu.with_memory_space_constraint(v, pltpu.HBM) for v in weights])


def gather(value):
    held = {0: value}
    k = lax.axis_size("chan") // 2
    while k:
        for j in list(held):
            held[j ^ k] = swap(held[j], "chan", k)
        k //= 2
    return [held[j] for j in sorted(held)]


def work(grad_out, feat_full, filters_full, upsample_weight, filters_half):
    n, m = lax.axis_size("chan"), lax.axis_size("grp")
    nx, ny, nz, ch = grad_out.shape
    half_x, half_y, half_z = nx // 2, n * ny // 2, nz // 2
    width = filters_half.shape[4]
    lanes = 27 * (ch // n)
    shape = jax.ShapeDtypeStruct
    edge = shape((HALO, ny, nz, ch), BF16)
    own, first, last = call(
        load_kernel,
        [shape((2 * nx, ny, nz, ch), BF16), edge, edge],
        [pltpu.SemaphoreType.DMA((4,))],
        (grad_out, feat_full),
        far=2,
    )
    from_left = shift(last, "grp", 1)
    from_right = shift(first, "grp", -1)
    bricks = gather(own)
    (rim,) = call(
        lambda *refs: rims_kernel(m, *refs),
        [shape((2 * HALO, ny, nz, ch), BF16)],
        [],
        (from_left, from_right),
    )
    rims = gather(rim)
    up = upsample_weight.shape[:3] + (width, ch)
    full, up = fetch((filters_full, upsample_weight), (filters_full.shape, up))
    keep, send = call(
        lambda *refs: taps_kernel(n, m, *refs),
        [shape((ch // 2, lanes), F32), shape((ch // 2, lanes), BF16)],
        [
            pltpu.VMEM((nx + 2, n * ny + 2, nz, ch), BF16),
            pltpu.VMEM((ch, lanes), F32),
        ],
        (*bricks, *rims),
    )
    got = swap(send, "grp", 1)
    chunk = (half_y // n, half_x, half_z, filters_half.shape[3])
    deep = nx + 2 * HALO
    chunks = call(
        lambda *refs: main_kernel(n, m, *refs),
        [shape(chunk, F32)] + [shape(chunk, BF16)] * (n - 1),
        [
            pltpu.VMEM((deep * ny, nz, ch), F32),
            pltpu.VMEM((4, deep // 2, n * ny + 2, nz, ch), BF16),
            pltpu.VMEM((3, half_y + 2, half_x + 2, half_z, width), F32),
            pltpu.VMEM((n,) + chunk, F32),
            pltpu.VMEM(filters_half.shape, BF16),
            pltpu.SemaphoreType.DMA,
        ],
        (*bricks, *rims, full, up, filters_half),
        far=1,
    )
    parts = [chunks[0]]
    for k in range(1, n):
        parts.append(swap(chunks[k], "chan", k))
    (grad_half,) = call(sum_kernel, [shape(chunk, BF16)], [], parts, False)
    for bit in range(1, m.bit_length() - 1):
        rows = keep.shape[0] // 2
        keep, send = call(
            lambda *refs: fold_kernel(bit, *refs),
            [shape((rows, lanes), F32), shape((rows, lanes), BF16)],
            [],
            (keep, got),
        )
        got = swap(send, "grp", 2**bit)
    (taps_grad,) = call(
        finish_kernel, [shape((3, 3, 3, ch // m, ch // n), F32)], [], (keep, got), False
    )
    return (grad_half, taps_grad)


def solution(mesh):
    in_specs = (
        P("grp", "chan", None, None),
        P("grp", "chan", None, None),
        P(),
        P(),
        P(None, None, None, None, "chan"),
    )
    out_specs = (P("chan", "grp", None, None), P(None, None, None, "grp", "chan"))
    return jax.shard_map(work, mesh=mesh, in_specs=in_specs, out_specs=out_specs, check_vma=False)
```

```python
import jax
import jax.numpy as jnp
from jax import lax
from jax.experimental import pallas as pl
from jax.experimental.pallas import tpu as pltpu
from jax.sharding import PartitionSpec as P


F32 = jnp.float32
BF16 = jnp.bfloat16
LIMIT = 20 * 2**20
HALO = 3
NT = (((1,), (1,)), ((), ()))
NN = (((1,), (0,)), ((), ()))


def dot(a, b, dims):
    return lax.dot_general(a, b, dims, preferred_element_type=F32)


def swap(value, axis, k):
    n = lax.axis_size(axis)
    return lax.ppermute(value, axis, [(i, i ^ k) for i in range(n)])


def shift(value, axis, step):
    n = lax.axis_size(axis)
    return lax.ppermute(value, axis, [(i, (i + step) % n) for i in range(n)])


def pair(k):
    return jnp.bitwise_xor(lax.axis_index("chan"), k)


def fetch_kernel(*refs):
    count = len(refs) // 2
    arrived = refs[2 * count]
    copies = []
    for k in range(count):
        source, target = refs[k], refs[count + k]
        if source.shape != target.shape:
            width = target.shape[3]
            start = pl.multiple_of(lax.axis_index("chan") * width, width)
            source = source.at[:, :, :, pl.ds(start, width), :]
        copies.append(pltpu.make_async_copy(source, target, arrived.at[k]))
    for copy in copies:
        copy.start()
    for copy in copies:
        copy.wait()


def spread_out(sources, full_ref, stage, spread):
    ny, nz, ch = sources[0][0].shape[1:]
    count = sum(source.shape[0] for source in sources[0])
    n, pairs, half_z = len(sources), count // 2, nz // 2
    rows = n * ny
    spread[:, :, 0] = jnp.zeros((4, pairs, nz, ch), BF16)
    spread[:, :, rows + 1] = jnp.zeros((4, pairs, nz, ch), BF16)
    level = lax.broadcasted_iota(jnp.int32, (count * ny, half_z, ch), 1)
    for k in range(n):
        at = 0
        for source in sources[k]:
            size = source.shape[0] * ny
            stage[at : at + size] = source.astype(F32).reshape(size, nz, ch)
            at += size
        even = stage[:, pl.ds(0, half_z, stride=2), :]
        odd = stage[:, pl.ds(1, half_z, stride=2), :]
        after = jnp.where(level == half_z - 1, 0.0, pltpu.roll(even, half_z - 1, 1))
        before = jnp.where(level == 0, 0.0, pltpu.roll(odd, 1, 1))
        first = pair(k) * ny + 1
        for which, value in enumerate((even, after, odd, before)):
            value = value.reshape(pairs, 2, ny, half_z, ch)
            for b in range(ny):
                packed = jnp.concatenate([value[:, 0, b], value[:, 1, b]], axis=1)
                spread[which, :, first + b] = packed.astype(BF16)
    taps = jnp.concatenate(
        [
            jnp.concatenate([full_ref[p, q, r] for q in range(3) for r in range(3)], axis=1)
            for p in range(3)
        ],
        axis=0,
    )
    products = []
    for order in ((2, 0, 3), (1, 2, 0)):
        window = jnp.concatenate(
            [
                spread[which, :, 2 - q : 2 - q + rows].reshape(pairs * rows * nz, ch)
                for q in range(3)
                for which in order
            ],
            axis=1,
        )
        products.append(dot(window, taps, NT).reshape(pairs, rows, 2, half_z, 3 * ch))
    return products


def inner_kernel(n, *refs):
    bricks, (full_ref, out_ref, stage, spread) = refs[:n], refs[n:]
    nx, ch = bricks[0].shape[0] // 2, bricks[0].shape[3]
    products = spread_out([[brick[:nx]] for brick in bricks], full_ref, stage, spread)
    for c, product in enumerate(products):
        for u in range(-1, nx + 1):
            total = None
            for p in range(3):
                x = u - p + 1
                if 0 <= x < nx:
                    term = product[x // 2, :, x % 2, :, p * ch : (p + 1) * ch]
                    total = term if total is None else total + term
            out_ref[c, u + 1] = total


def main_kernel(n, m, *refs):
    rims, (inner_ref, full_ref, up_ref, half_ref) = refs[:n], refs[n : n + 4]
    outs, (stage, spread, padded, result, held, arrived) = (
        refs[n + 4 : 2 * n + 4],
        refs[2 * n + 4 :],
    )
    load = pltpu.make_async_copy(half_ref, held, arrived)
    load.start()
    halo = rims[0].shape[0] // 2 - 1
    nx, rows, half_z, ch = inner_ref.shape[1:]
    nx = nx - 2
    half_x, half_y = nx // 2, rows // 2
    width = up_ref.shape[3]
    products = spread_out([[rim[: 2 * halo]] for rim in rims], full_ref, stage, spread)
    grads = []
    for c, product in enumerate(products):
        planes = {}
        for u in range(-2, nx + 2):
            total = inner_ref[c, u + 1] if -1 <= u <= nx else None
            for p in range(3):
                x = u - p + 1
                if not 0 <= x < nx:
                    at = x + halo if x < 0 else x - nx + halo
                    term = product[at // 2, :, at % 2, :, p * ch : (p + 1) * ch]
                    total = term if total is None else total + term
            planes[u] = total.reshape(half_y, 2, half_z, ch)
        grads.append(planes)
    columns = []
    for a in range(2):
        for b in range(2):
            for c in range(2):
                pieces = [
                    grads[c][2 * i + a][:, b].reshape(half_y * half_z, ch)
                    for i in range(-1, half_x + 1)
                ]
                columns.append(jnp.concatenate(pieces, axis=0).astype(BF16))
    up = jnp.concatenate(
        [up_ref[a, b, c] for a in range(2) for b in range(2) for c in range(2)], axis=1
    )
    wide_x = half_x + 2
    coarse = dot(jnp.concatenate(columns, axis=1), up, NT).reshape(wide_x, half_y, half_z, width)
    g = lax.axis_index("grp")
    low = jnp.where(g > 0, 1.0, 0.0)
    high = jnp.where(g < m - 1, 1.0, 0.0)
    padded[:, 0] = jnp.zeros((3, wide_x, half_z, width), F32)
    padded[:, half_y + 1] = jnp.zeros((3, wide_x, half_z, width), F32)
    level = lax.broadcasted_iota(jnp.int32, (half_y, half_z, width), 1)
    for i in range(wide_x):
        plane = coarse[i]
        if i == 0:
            plane = plane * low
        if i == wide_x - 1:
            plane = plane * high
        plane = plane.astype(BF16).astype(F32)
        padded[0, 1 : half_y + 1, i] = jnp.where(
            level == half_z - 1, 0.0, pltpu.roll(plane, half_z - 1, 1)
        )
        padded[1, 1 : half_y + 1, i] = plane
        padded[2, 1 : half_y + 1, i] = jnp.where(level == 0, 0.0, pltpu.roll(plane, 1, 1))
    cells = half_y * half_x * half_z
    total = None
    load.wait()
    for p in range(3):
        windows = [
            padded[r, 2 - q : 2 - q + half_y, 2 - p : 2 - p + half_x]
            .reshape(cells, width)
            .astype(BF16)
            for q in range(3)
            for r in range(3)
        ]
        kernels = [held[p, q, r] for q in range(3) for r in range(3)]
        if width % 128 == 0:
            windows = [jnp.concatenate(windows, axis=1)]
            kernels = [jnp.concatenate(kernels, axis=1)]
        for window, kernel in zip(windows, kernels):
            product = dot(window, kernel, NT)
            total = product if total is None else total + product
    result[...] = total.reshape(result.shape)
    for k in range(n):
        outs[k][...] = result[pair(k)].astype(outs[k].dtype)


def chosen_lanes(cells, pick, part, nz):
    chosen = dot(cells, pick, NN)
    level = lax.rem(lax.broadcasted_iota(jnp.int32, chosen.shape, 0), nz)
    lane = lax.broadcasted_iota(jnp.int32, chosen.shape, 1)
    count = chosen.shape[0]
    above = jnp.where(level == nz - 1, 0.0, pltpu.roll(chosen, count - 1, 0))
    below = jnp.where(level == 0, 0.0, pltpu.roll(chosen, 1, 0))
    mixed = jnp.where(lane < part, above, jnp.where(lane < 2 * part, chosen, below))
    return mixed.astype(BF16)


def selections(n, m, ch):
    part, block = ch // n, ch // m
    start = lax.axis_index("chan") * part
    source = lax.broadcasted_iota(jnp.int32, (ch, ch), 0)
    target = lax.broadcasted_iota(jnp.int32, (ch, ch), 1)
    copies = (lax.rem(target, part) + start == source) & (target < 3 * part)
    pick = jnp.where(copies, 1.0, 0.0).astype(BF16)
    bits = m.bit_length() - 1
    owner = target // block
    turned = jnp.zeros_like(owner)
    for bit in range(bits):
        turned = turned + (owner // 2**bit % 2) * 2 ** (bits - 1 - bit)
    place = turned * block + lax.rem(target, block)
    return pick, place, source


def taps_kernel(n, m, *refs):
    bricks, (keep_ref, send_ref, spread, table) = refs[:n], refs[n:]
    nx, ny, nz, ch = bricks[0].shape
    nx = nx // 2
    rows = n * ny
    part = ch // n
    cells = nx * ny * nz
    spread[:, 0] = jnp.zeros((nx, nz, ch), BF16)
    spread[:, rows + 1] = jnp.zeros((nx, nz, ch), BF16)
    pick, place, source = selections(n, m, ch)
    order = jnp.where(place == source, 1.0, 0.0).astype(BF16)
    turned_feats = []
    for k in range(n):
        mixed = chosen_lanes(bricks[k][:nx].reshape(cells, ch), pick, part, nz)
        mixed = mixed.reshape(nx, ny, nz, ch)
        first = pair(k) * ny + 1
        for b in range(ny):
            spread[:, first + b] = mixed[:, b]
        turned_feats.append(dot(order, bricks[k][nx:].reshape(cells, ch), NT).astype(BF16))
    totals = []
    plane = ny * nz
    for p in range(3):
        total = None
        feat_from, grad_from = max(0, p - 1), max(0, 1 - p)
        count = nx - abs(p - 1)
        for k in range(n):
            first = pair(k) * ny
            window = jnp.concatenate(
                [
                    spread[
                        grad_from : grad_from + count, pl.ds(first + 2 - q, ny)
                    ].reshape(count * plane, ch)
                    for q in range(3)
                ],
                axis=1,
            )
            feat = turned_feats[k][:, feat_from * plane : (feat_from + count) * plane]
            product = dot(feat, window, NN)
            total = product if total is None else total + product
        totals += [total[:, q * ch : q * ch + 3 * part] for q in range(3)]
    table[...] = jnp.concatenate(totals, axis=1)
    half = ch // 2
    bit = lax.rem(lax.axis_index("grp"), 2)
    keep_ref[...] = table[pl.ds(pl.multiple_of(bit * half, half), half), :]
    send_ref[...] = table[pl.ds(pl.multiple_of((1 - bit) * half, half), half), :].astype(BF16)


def outer_kernel(n, m, *refs):
    bricks, rims, (out_ref, spread) = refs[:n], refs[n : 2 * n], refs[2 * n :]
    nx, ny, nz, ch = bricks[0].shape
    nx = nx // 2
    halo = rims[0].shape[0] // 2 - 1
    rows = n * ny
    part = ch // n
    plane = ny * nz
    half = ch // 2
    spread[:, 0] = jnp.zeros((4, nz, ch), BF16)
    spread[:, rows + 1] = jnp.zeros((4, nz, ch), BF16)
    pick, place, source = selections(n, m, ch)
    bit = lax.rem(lax.axis_index("grp"), 2)
    order = jnp.where(place[:half] == source[:half] + bit * half, 1.0, 0.0).astype(BF16)
    cells = []
    for k in range(n):
        for planes in (
            bricks[k][0:1],
            rims[k][halo : halo + 1],
            rims[k][halo - 1 : halo],
            bricks[k][nx - 1 : nx],
        ):
            cells.append(planes.reshape(plane, ch))
    mixed = chosen_lanes(jnp.concatenate(cells, axis=0), pick, part, nz)
    mixed = mixed.reshape(n, 4, ny, nz, ch)
    for k in range(n):
        first = pair(k) * ny + 1
        for b in range(ny):
            spread[:, first + b] = mixed[k, :, b]
    for e in range(2):
        feats, windows = [], []
        for k in range(n):
            if e == 0:
                sides = (rims[k][2 * halo], bricks[k][2 * nx - 1])
            else:
                sides = (bricks[k][nx], rims[k][2 * halo + 1])
            first = pair(k) * ny
            for side, feat in enumerate(sides):
                feats.append(feat.reshape(plane, ch))
                windows.append(
                    jnp.concatenate(
                        [
                            spread[2 * e + side, pl.ds(first + 2 - q, ny)].reshape(plane, ch)
                            for q in range(3)
                        ],
                        axis=1,
                    )
                )
        feat = dot(order, jnp.concatenate(feats, axis=0), NT).astype(BF16)
        total = dot(feat, jnp.concatenate(windows, axis=0), NN)
        out_ref[e] = jnp.concatenate(
            [total[:, q * ch : q * ch + 3 * part] for q in range(3)], axis=1
        )


def load_kernel(grad_ref, feat_ref, own_ref, first_ref, last_ref, arrived):
    nx = grad_ref.shape[0]
    halo = first_ref.shape[0] - 1
    cut = pl.ds(0, halo)
    copies = [
        pltpu.make_async_copy(
            grad_ref.at[pl.ds(nx - halo, halo)], last_ref.at[cut], arrived.at[0]
        ),
        pltpu.make_async_copy(grad_ref.at[cut], first_ref.at[cut], arrived.at[1]),
        pltpu.make_async_copy(feat_ref.at[nx - 1], last_ref.at[halo], arrived.at[4]),
        pltpu.make_async_copy(feat_ref.at[0], first_ref.at[halo], arrived.at[5]),
        pltpu.make_async_copy(grad_ref, own_ref.at[pl.ds(0, nx)], arrived.at[2]),
        pltpu.make_async_copy(feat_ref, own_ref.at[pl.ds(nx, nx)], arrived.at[3]),
    ]
    for copy in copies:
        copy.start()
    for copy in copies:
        copy.wait()


def rims_kernel(m, left_ref, right_ref, out_ref):
    g = lax.axis_index("grp")
    halo = left_ref.shape[0] - 1
    left, right = left_ref[...], right_ref[...]
    left = jnp.where(g > 0, left, jnp.zeros_like(left))
    right = jnp.where(g < m - 1, right, jnp.zeros_like(right))
    out_ref[:halo] = left[:halo]
    out_ref[halo : 2 * halo] = right[:halo]
    out_ref[2 * halo] = left[halo]
    out_ref[2 * halo + 1] = right[halo]


def fold_kernel(bit, keep_ref, got_ref, *refs):
    extra, (held_ref, send_ref) = refs[:-2], refs[-2:]
    total = keep_ref[...] + got_ref[...].astype(F32)
    if extra:
        (outer_ref,) = extra
        third = outer_ref.shape[2]
        total = jnp.concatenate(
            [
                total[:, :third] + outer_ref[0],
                total[:, third : 2 * third],
                total[:, 2 * third :] + outer_ref[1],
            ],
            axis=1,
        )
    half = held_ref.shape[0]
    upper = lax.rem(lax.axis_index("grp") // 2**bit, 2) == 1
    held_ref[...] = jnp.where(upper, total[half:], total[:half])
    send_ref[...] = jnp.where(upper, total[:half], total[half:]).astype(BF16)


def finish_kernel(keep_ref, got_ref, out_ref):
    part = out_ref.shape[4]
    total = keep_ref[...] + got_ref[...].astype(F32)
    for p in range(3):
        for q in range(3):
            for r in range(3):
                at = (9 * p + 3 * q + r) * part
                out_ref[p, q, r] = total[:, at : at + part]


def sum_kernel(*refs):
    inputs, out_ref = refs[:-1], refs[-1]
    total = inputs[0][...]
    for ref in inputs[1:]:
        total = total + ref[...].astype(F32)
    out_ref[...] = total.astype(BF16)


def call(kernel, outs, scratch, inputs, placed=True, far=0):
    spaces = [pltpu.VMEM] * (len(inputs) - far) + [pltpu.HBM] * far
    return pl.pallas_call(
        kernel,
        out_shape=[pltpu.VMEM(v.shape, v.dtype) if placed else v for v in outs],
        in_specs=[pl.BlockSpec(memory_space=space) for space in spaces],
        out_specs=[pl.BlockSpec(memory_space=pltpu.VMEM)] * len(outs),
        scratch_shapes=scratch,
        compiler_params=pltpu.CompilerParams(vmem_limit_bytes=LIMIT),
    )(*[pltpu.with_memory_space_constraint(v, space) for v, space in zip(inputs, spaces)])


def fetch(weights, shapes):
    count = len(weights)
    return pl.pallas_call(
        fetch_kernel,
        out_shape=[pltpu.VMEM(shape, BF16) for shape in shapes],
        in_specs=[pl.BlockSpec(memory_space=pltpu.HBM)] * count,
        out_specs=[pl.BlockSpec(memory_space=pltpu.VMEM)] * count,
        scratch_shapes=[pltpu.SemaphoreType.DMA((count,))],
        compiler_params=pltpu.CompilerParams(vmem_limit_bytes=LIMIT),
    )(*[pltpu.with_memory_space_constraint(v, pltpu.HBM) for v in weights])


def gather(value):
    held = {0: value}
    k = lax.axis_size("chan") // 2
    while k:
        for j in list(held):
            held[j ^ k] = swap(held[j], "chan", k)
        k //= 2
    return [held[j] for j in sorted(held)]


def work(grad_out, feat_full, filters_full, upsample_weight, filters_half):
    n, m = lax.axis_size("chan"), lax.axis_size("grp")
    nx, ny, nz, ch = grad_out.shape
    half_x, half_y, half_z = nx // 2, n * ny // 2, nz // 2
    width = filters_half.shape[4]
    lanes = 27 * (ch // n)
    shape = jax.ShapeDtypeStruct
    edge = shape((HALO + 1, ny, nz, ch), BF16)
    own, first, last = call(
        load_kernel,
        [shape((2 * nx, ny, nz, ch), BF16), edge, edge],
        [pltpu.SemaphoreType.DMA((6,))],
        (grad_out, feat_full),
        far=2,
    )
    from_left = shift(last, "grp", 1)
    from_right = shift(first, "grp", -1)
    bricks = gather(own)
    (rim,) = call(
        lambda *refs: rims_kernel(m, *refs),
        [shape((2 * HALO + 2, ny, nz, ch), BF16)],
        [],
        (from_left, from_right),
    )
    rims = gather(rim)
    up = upsample_weight.shape[:3] + (width, ch)
    full, up = fetch((filters_full, upsample_weight), (filters_full.shape, up))
    keep, send = call(
        lambda *refs: taps_kernel(n, m, *refs),
        [shape((ch // 2, lanes), F32), shape((ch // 2, lanes), BF16)],
        [pltpu.VMEM((nx, n * ny + 2, nz, ch), BF16), pltpu.VMEM((ch, lanes), F32)],
        tuple(bricks),
    )
    (outer,) = call(
        lambda *refs: outer_kernel(n, m, *refs),
        [shape((2, ch // 2, lanes // 3), F32)],
        [pltpu.VMEM((4, n * ny + 2, nz, ch), BF16)],
        (*bricks, *rims),
    )
    got = swap(send, "grp", 1)
    (inner,) = call(
        lambda *refs: inner_kernel(n, *refs),
        [shape((2, nx + 2, n * ny, half_z, ch), F32)],
        [
            pltpu.VMEM((nx * ny, nz, ch), F32),
            pltpu.VMEM((4, half_x, n * ny + 2, nz, ch), BF16),
        ],
        (*bricks, full),
    )
    chunk = (half_y // n, half_x, half_z, filters_half.shape[3])
    chunks = call(
        lambda *refs: main_kernel(n, m, *refs),
        [shape(chunk, F32)] + [shape(chunk, BF16)] * (n - 1),
        [
            pltpu.VMEM((2 * HALO * ny, nz, ch), F32),
            pltpu.VMEM((4, HALO, n * ny + 2, nz, ch), BF16),
            pltpu.VMEM((3, half_y + 2, half_x + 2, half_z, width), F32),
            pltpu.VMEM((n,) + chunk, F32),
            pltpu.VMEM(filters_half.shape, BF16),
            pltpu.SemaphoreType.DMA,
        ],
        (*rims, inner, full, up, filters_half),
        far=1,
    )
    parts = [chunks[0]]
    for k in range(1, n):
        parts.append(swap(chunks[k], "chan", k))
    (grad_half,) = call(sum_kernel, [shape(chunk, BF16)], [], parts, False)
    for bit in range(1, m.bit_length() - 1):
        rows = keep.shape[0] // 2
        keep, send = call(
            lambda *refs: fold_kernel(bit, *refs),
            [shape((rows, lanes), F32), shape((rows, lanes), BF16)],
            [],
            (keep, got) if bit > 1 else (keep, got, outer),
        )
        got = swap(send, "grp", 2**bit)
    (taps_grad,) = call(
        finish_kernel, [shape((3, 3, 3, ch // m, ch // n), F32)], [], (keep, got), False
    )
    return (grad_half, taps_grad)


def solution(mesh):
    in_specs = (
        P("grp", "chan", None, None),
        P("grp", "chan", None, None),
        P(),
        P(),
        P(None, None, None, None, "chan"),
    )
    out_specs = (P("chan", "grp", None, None), P(None, None, None, "grp", "chan"))
    return jax.shard_map(work, mesh=mesh, in_specs=in_specs, out_specs=out_specs, check_vma=False)
```

```python
import jax
import jax.numpy as jnp
from jax import lax
from jax.experimental import pallas as pl
from jax.experimental.pallas import tpu as pltpu
from jax.sharding import PartitionSpec as P


F32 = jnp.float32
BF16 = jnp.bfloat16
LIMIT = 20 * 2**20
HALO = 3
NT = (((1,), (1,)), ((), ()))
NN = (((1,), (0,)), ((), ()))


def dot(a, b, dims):
    return lax.dot_general(a, b, dims, preferred_element_type=F32)


def swap(value, axis, k):
    n = lax.axis_size(axis)
    return lax.ppermute(value, axis, [(i, i ^ k) for i in range(n)])


def shift(value, axis, step):
    n = lax.axis_size(axis)
    return lax.ppermute(value, axis, [(i, (i + step) % n) for i in range(n)])


def pair(k):
    return jnp.bitwise_xor(lax.axis_index("chan"), k)


def fetch_kernel(*refs):
    count = len(refs) // 2
    arrived = refs[2 * count]
    copies = []
    for k in range(count):
        source, target = refs[k], refs[count + k]
        if source.shape != target.shape:
            width = target.shape[3]
            start = pl.multiple_of(lax.axis_index("chan") * width, width)
            source = source.at[:, :, :, pl.ds(start, width), :]
        copies.append(pltpu.make_async_copy(source, target, arrived.at[k]))
    for copy in copies:
        copy.start()
    for copy in copies:
        copy.wait()


def spread_out(sources, full_ref, stage, spread):
    ny, nz, ch = sources[0][0].shape[1:]
    count = sum(source.shape[0] for source in sources[0])
    n, pairs, half_z = len(sources), count // 2, nz // 2
    rows = n * ny
    spread[:, :, 0] = jnp.zeros((4, pairs, nz, ch), BF16)
    spread[:, :, rows + 1] = jnp.zeros((4, pairs, nz, ch), BF16)
    level = lax.broadcasted_iota(jnp.int32, (count * ny, half_z, ch), 1)
    for k in range(n):
        at = 0
        for source in sources[k]:
            size = source.shape[0] * ny
            stage[at : at + size] = source.astype(F32).reshape(size, nz, ch)
            at += size
        even = stage[:, pl.ds(0, half_z, stride=2), :]
        odd = stage[:, pl.ds(1, half_z, stride=2), :]
        after = jnp.where(level == half_z - 1, 0.0, pltpu.roll(even, half_z - 1, 1))
        before = jnp.where(level == 0, 0.0, pltpu.roll(odd, 1, 1))
        first = pair(k) * ny + 1
        for which, value in enumerate((even, after, odd, before)):
            value = value.reshape(pairs, 2, ny, half_z, ch)
            for b in range(ny):
                packed = jnp.concatenate([value[:, 0, b], value[:, 1, b]], axis=1)
                spread[which, :, first + b] = packed.astype(BF16)
    taps = jnp.concatenate(
        [
            jnp.concatenate([full_ref[p, q, r] for q in range(3) for r in range(3)], axis=1)
            for p in range(3)
        ],
        axis=0,
    )
    products = []
    for order in ((2, 0, 3), (1, 2, 0)):
        window = jnp.concatenate(
            [
                spread[which, :, 2 - q : 2 - q + rows].reshape(pairs * rows * nz, ch)
                for q in range(3)
                for which in order
            ],
            axis=1,
        )
        products.append(dot(window, taps, NT).reshape(pairs, rows, 2, half_z, 3 * ch))
    return products


def inner_kernel(n, *refs):
    bricks, (full_ref, out_ref, stage, spread) = refs[:n], refs[n:]
    nx, ch = bricks[0].shape[0] // 2, bricks[0].shape[3]
    products = spread_out([[brick[:nx]] for brick in bricks], full_ref, stage, spread)
    for c, product in enumerate(products):
        for u in range(-1, nx + 1):
            total = None
            for p in range(3):
                x = u - p + 1
                if 0 <= x < nx:
                    term = product[x // 2, :, x % 2, :, p * ch : (p + 1) * ch]
                    total = term if total is None else total + term
            out_ref[c, u + 1] = total


def main_kernel(n, m, *refs):
    rims, (inner_ref, full_ref, up_ref, half_ref) = refs[:n], refs[n : n + 4]
    outs, (stage, spread, padded, result, held, arrived) = (
        refs[n + 4 : 2 * n + 4],
        refs[2 * n + 4 :],
    )
    loads = [
        pltpu.make_async_copy(half_ref.at[p], held.at[p], arrived.at[p]) for p in range(3)
    ]
    for load in loads:
        load.start()
    halo = rims[0].shape[0] // 2 - 1
    nx, rows, half_z, ch = inner_ref.shape[1:]
    nx = nx - 2
    half_x, half_y = nx // 2, rows // 2
    width = up_ref.shape[3]
    products = spread_out([[rim[: 2 * halo]] for rim in rims], full_ref, stage, spread)
    grads = []
    for c, product in enumerate(products):
        planes = {}
        for u in range(-2, nx + 2):
            total = inner_ref[c, u + 1] if -1 <= u <= nx else None
            for p in range(3):
                x = u - p + 1
                if not 0 <= x < nx:
                    at = x + halo if x < 0 else x - nx + halo
                    term = product[at // 2, :, at % 2, :, p * ch : (p + 1) * ch]
                    total = term if total is None else total + term
            planes[u] = total.reshape(half_y, 2, half_z, ch)
        grads.append(planes)
    columns = []
    for a in range(2):
        for b in range(2):
            for c in range(2):
                pieces = [
                    grads[c][2 * i + a][:, b].reshape(half_y * half_z, ch)
                    for i in range(-1, half_x + 1)
                ]
                columns.append(jnp.concatenate(pieces, axis=0).astype(BF16))
    up = jnp.concatenate(
        [up_ref[a, b, c] for a in range(2) for b in range(2) for c in range(2)], axis=1
    )
    wide_x = half_x + 2
    coarse = dot(jnp.concatenate(columns, axis=1), up, NT).reshape(wide_x, half_y, half_z, width)
    g = lax.axis_index("grp")
    low = jnp.where(g > 0, 1.0, 0.0)
    high = jnp.where(g < m - 1, 1.0, 0.0)
    padded[:, 0] = jnp.zeros((3, wide_x, half_z, width), F32)
    padded[:, half_y + 1] = jnp.zeros((3, wide_x, half_z, width), F32)
    level = lax.broadcasted_iota(jnp.int32, (half_y, half_z, width), 1)
    for i in range(wide_x):
        plane = coarse[i]
        if i == 0:
            plane = plane * low
        if i == wide_x - 1:
            plane = plane * high
        plane = plane.astype(BF16).astype(F32)
        padded[0, 1 : half_y + 1, i] = jnp.where(
            level == half_z - 1, 0.0, pltpu.roll(plane, half_z - 1, 1)
        )
        padded[1, 1 : half_y + 1, i] = plane
        padded[2, 1 : half_y + 1, i] = jnp.where(level == 0, 0.0, pltpu.roll(plane, 1, 1))
    cells = half_y * half_x * half_z
    total = None
    for p in range(3):
        loads[p].wait()
        windows = [
            padded[r, 2 - q : 2 - q + half_y, 2 - p : 2 - p + half_x]
            .reshape(cells, width)
            .astype(BF16)
            for q in range(3)
            for r in range(3)
        ]
        kernels = [held[p, q, r] for q in range(3) for r in range(3)]
        if width % 128 == 0:
            windows = [jnp.concatenate(windows, axis=1)]
            kernels = [jnp.concatenate(kernels, axis=1)]
        for window, kernel in zip(windows, kernels):
            product = dot(window, kernel, NT)
            total = product if total is None else total + product
    result[...] = total.reshape(result.shape)
    for k in range(n):
        outs[k][...] = result[pair(k)].astype(outs[k].dtype)


def chosen_lanes(cells, pick, part, nz):
    chosen = dot(cells, pick, NN)
    level = lax.rem(lax.broadcasted_iota(jnp.int32, chosen.shape, 0), nz)
    lane = lax.broadcasted_iota(jnp.int32, chosen.shape, 1)
    count = chosen.shape[0]
    above = jnp.where(level == nz - 1, 0.0, pltpu.roll(chosen, count - 1, 0))
    below = jnp.where(level == 0, 0.0, pltpu.roll(chosen, 1, 0))
    mixed = jnp.where(lane < part, above, jnp.where(lane < 2 * part, chosen, below))
    return mixed.astype(BF16)


def selections(n, m, ch):
    part, block = ch // n, ch // m
    start = lax.axis_index("chan") * part
    source = lax.broadcasted_iota(jnp.int32, (ch, ch), 0)
    target = lax.broadcasted_iota(jnp.int32, (ch, ch), 1)
    copies = (lax.rem(target, part) + start == source) & (target < 3 * part)
    pick = jnp.where(copies, 1.0, 0.0).astype(BF16)
    bits = m.bit_length() - 1
    owner = target // block
    turned = jnp.zeros_like(owner)
    for bit in range(bits):
        turned = turned + (owner // 2**bit % 2) * 2 ** (bits - 1 - bit)
    place = turned * block + lax.rem(target, block)
    return pick, place, source


def taps_kernel(n, m, *refs):
    bricks, (keep_ref, send_ref, spread, table) = refs[:n], refs[n:]
    nx, ny, nz, ch = bricks[0].shape
    nx = nx // 2
    rows = n * ny
    part = ch // n
    cells = nx * ny * nz
    spread[:, 0] = jnp.zeros((nx, nz, ch), BF16)
    spread[:, rows + 1] = jnp.zeros((nx, nz, ch), BF16)
    pick, place, source = selections(n, m, ch)
    order = jnp.where(place == source, 1.0, 0.0).astype(BF16)
    turned_feats = []
    for k in range(n):
        mixed = chosen_lanes(bricks[k][:nx].reshape(cells, ch), pick, part, nz)
        mixed = mixed.reshape(nx, ny, nz, ch)
        first = pair(k) * ny + 1
        for b in range(ny):
            spread[:, first + b] = mixed[:, b]
        turned_feats.append(dot(order, bricks[k][nx:].reshape(cells, ch), NT).astype(BF16))
    totals = []
    plane = ny * nz
    for p in range(3):
        total = None
        feat_from, grad_from = max(0, p - 1), max(0, 1 - p)
        count = nx - abs(p - 1)
        for k in range(n):
            first = pair(k) * ny
            window = jnp.concatenate(
                [
                    spread[
                        grad_from : grad_from + count, pl.ds(first + 2 - q, ny)
                    ].reshape(count * plane, ch)
                    for q in range(3)
                ],
                axis=1,
            )
            feat = turned_feats[k][:, feat_from * plane : (feat_from + count) * plane]
            product = dot(feat, window, NN)
            total = product if total is None else total + product
        totals += [total[:, q * ch : q * ch + 3 * part] for q in range(3)]
    table[...] = jnp.concatenate(totals, axis=1)
    half = ch // 2
    bit = lax.rem(lax.axis_index("grp"), 2)
    keep_ref[...] = table[pl.ds(pl.multiple_of(bit * half, half), half), :]
    send_ref[...] = table[pl.ds(pl.multiple_of((1 - bit) * half, half), half), :].astype(BF16)


def outer_kernel(n, m, *refs):
    bricks, rims, (out_ref, spread) = refs[:n], refs[n : 2 * n], refs[2 * n :]
    nx, ny, nz, ch = bricks[0].shape
    nx = nx // 2
    halo = rims[0].shape[0] // 2 - 1
    rows = n * ny
    part = ch // n
    plane = ny * nz
    half = ch // 2
    spread[:, 0] = jnp.zeros((4, nz, ch), BF16)
    spread[:, rows + 1] = jnp.zeros((4, nz, ch), BF16)
    pick, place, source = selections(n, m, ch)
    bit = lax.rem(lax.axis_index("grp"), 2)
    order = jnp.where(place[:half] == source[:half] + bit * half, 1.0, 0.0).astype(BF16)
    cells = []
    for k in range(n):
        for planes in (
            bricks[k][0:1],
            rims[k][halo : halo + 1],
            rims[k][halo - 1 : halo],
            bricks[k][nx - 1 : nx],
        ):
            cells.append(planes.reshape(plane, ch))
    mixed = chosen_lanes(jnp.concatenate(cells, axis=0), pick, part, nz)
    mixed = mixed.reshape(n, 4, ny, nz, ch)
    for k in range(n):
        first = pair(k) * ny + 1
        for b in range(ny):
            spread[:, first + b] = mixed[k, :, b]
    for e in range(2):
        feats, windows = [], []
        for k in range(n):
            if e == 0:
                sides = (rims[k][2 * halo], bricks[k][2 * nx - 1])
            else:
                sides = (bricks[k][nx], rims[k][2 * halo + 1])
            first = pair(k) * ny
            for side, feat in enumerate(sides):
                feats.append(feat.reshape(plane, ch))
                windows.append(
                    jnp.concatenate(
                        [
                            spread[2 * e + side, pl.ds(first + 2 - q, ny)].reshape(plane, ch)
                            for q in range(3)
                        ],
                        axis=1,
                    )
                )
        feat = dot(order, jnp.concatenate(feats, axis=0), NT).astype(BF16)
        total = dot(feat, jnp.concatenate(windows, axis=0), NN)
        out_ref[e] = jnp.concatenate(
            [total[:, q * ch : q * ch + 3 * part] for q in range(3)], axis=1
        )


def load_kernel(grad_ref, feat_ref, own_ref, first_ref, last_ref, arrived):
    nx = grad_ref.shape[0]
    halo = first_ref.shape[0] - 1
    cut = pl.ds(0, halo)
    copies = [
        pltpu.make_async_copy(
            grad_ref.at[pl.ds(nx - halo, halo)], last_ref.at[cut], arrived.at[0]
        ),
        pltpu.make_async_copy(grad_ref.at[cut], first_ref.at[cut], arrived.at[1]),
        pltpu.make_async_copy(feat_ref.at[nx - 1], last_ref.at[halo], arrived.at[4]),
        pltpu.make_async_copy(feat_ref.at[0], first_ref.at[halo], arrived.at[5]),
        pltpu.make_async_copy(grad_ref, own_ref.at[pl.ds(0, nx)], arrived.at[2]),
        pltpu.make_async_copy(feat_ref, own_ref.at[pl.ds(nx, nx)], arrived.at[3]),
    ]
    for copy in copies:
        copy.start()
    for copy in copies:
        copy.wait()


def rims_kernel(m, left_ref, right_ref, out_ref):
    g = lax.axis_index("grp")
    halo = left_ref.shape[0] - 1
    left, right = left_ref[...], right_ref[...]
    left = jnp.where(g > 0, left, jnp.zeros_like(left))
    right = jnp.where(g < m - 1, right, jnp.zeros_like(right))
    out_ref[:halo] = left[:halo]
    out_ref[halo : 2 * halo] = right[:halo]
    out_ref[2 * halo] = left[halo]
    out_ref[2 * halo + 1] = right[halo]


def fold_kernel(bit, keep_ref, got_ref, *refs):
    extra, (held_ref, send_ref) = refs[:-2], refs[-2:]
    total = keep_ref[...] + got_ref[...].astype(F32)
    if extra:
        (outer_ref,) = extra
        third = outer_ref.shape[2]
        total = jnp.concatenate(
            [
                total[:, :third] + outer_ref[0],
                total[:, third : 2 * third],
                total[:, 2 * third :] + outer_ref[1],
            ],
            axis=1,
        )
    half = held_ref.shape[0]
    upper = lax.rem(lax.axis_index("grp") // 2**bit, 2) == 1
    held_ref[...] = jnp.where(upper, total[half:], total[:half])
    send_ref[...] = jnp.where(upper, total[:half], total[half:]).astype(BF16)


def finish_kernel(keep_ref, got_ref, out_ref):
    part = out_ref.shape[4]
    total = keep_ref[...] + got_ref[...].astype(F32)
    for p in range(3):
        for q in range(3):
            for r in range(3):
                at = (9 * p + 3 * q + r) * part
                out_ref[p, q, r] = total[:, at : at + part]


def sum_kernel(*refs):
    inputs, out_ref = refs[:-1], refs[-1]
    total = inputs[0][...]
    for ref in inputs[1:]:
        total = total + ref[...].astype(F32)
    out_ref[...] = total.astype(BF16)


def call(kernel, outs, scratch, inputs, placed=True, far=0):
    spaces = [pltpu.VMEM] * (len(inputs) - far) + [pltpu.HBM] * far
    return pl.pallas_call(
        kernel,
        out_shape=[pltpu.VMEM(v.shape, v.dtype) if placed else v for v in outs],
        in_specs=[pl.BlockSpec(memory_space=space) for space in spaces],
        out_specs=[pl.BlockSpec(memory_space=pltpu.VMEM)] * len(outs),
        scratch_shapes=scratch,
        compiler_params=pltpu.CompilerParams(vmem_limit_bytes=LIMIT),
    )(*[pltpu.with_memory_space_constraint(v, space) for v, space in zip(inputs, spaces)])


def fetch(weights, shapes):
    count = len(weights)
    return pl.pallas_call(
        fetch_kernel,
        out_shape=[pltpu.VMEM(shape, BF16) for shape in shapes],
        in_specs=[pl.BlockSpec(memory_space=pltpu.HBM)] * count,
        out_specs=[pl.BlockSpec(memory_space=pltpu.VMEM)] * count,
        scratch_shapes=[pltpu.SemaphoreType.DMA((count,))],
        compiler_params=pltpu.CompilerParams(vmem_limit_bytes=LIMIT),
    )(*[pltpu.with_memory_space_constraint(v, pltpu.HBM) for v in weights])


def gather(value):
    held = {0: value}
    k = lax.axis_size("chan") // 2
    while k:
        for j in list(held):
            held[j ^ k] = swap(held[j], "chan", k)
        k //= 2
    return [held[j] for j in sorted(held)]


def work(grad_out, feat_full, filters_full, upsample_weight, filters_half):
    n, m = lax.axis_size("chan"), lax.axis_size("grp")
    nx, ny, nz, ch = grad_out.shape
    half_x, half_y, half_z = nx // 2, n * ny // 2, nz // 2
    width = filters_half.shape[4]
    lanes = 27 * (ch // n)
    shape = jax.ShapeDtypeStruct
    edge = shape((HALO + 1, ny, nz, ch), BF16)
    own, first, last = call(
        load_kernel,
        [shape((2 * nx, ny, nz, ch), BF16), edge, edge],
        [pltpu.SemaphoreType.DMA((6,))],
        (grad_out, feat_full),
        far=2,
    )
    from_left = shift(last, "grp", 1)
    from_right = shift(first, "grp", -1)
    bricks = gather(own)
    (rim,) = call(
        lambda *refs: rims_kernel(m, *refs),
        [shape((2 * HALO + 2, ny, nz, ch), BF16)],
        [],
        (from_left, from_right),
    )
    rims = gather(rim)
    up = upsample_weight.shape[:3] + (width, ch)
    full, up = fetch((filters_full, upsample_weight), (filters_full.shape, up))
    keep, send = call(
        lambda *refs: taps_kernel(n, m, *refs),
        [shape((ch // 2, lanes), F32), shape((ch // 2, lanes), BF16)],
        [pltpu.VMEM((nx, n * ny + 2, nz, ch), BF16), pltpu.VMEM((ch, lanes), F32)],
        tuple(bricks),
    )
    (outer,) = call(
        lambda *refs: outer_kernel(n, m, *refs),
        [shape((2, ch // 2, lanes // 3), F32)],
        [pltpu.VMEM((4, n * ny + 2, nz, ch), BF16)],
        (*bricks, *rims),
    )
    got = swap(send, "grp", 1)
    (inner,) = call(
        lambda *refs: inner_kernel(n, *refs),
        [shape((2, nx + 2, n * ny, half_z, ch), F32)],
        [
            pltpu.VMEM((nx * ny, nz, ch), F32),
            pltpu.VMEM((4, half_x, n * ny + 2, nz, ch), BF16),
        ],
        (*bricks, full),
    )
    chunk = (half_y // n, half_x, half_z, filters_half.shape[3])
    chunks = call(
        lambda *refs: main_kernel(n, m, *refs),
        [shape(chunk, F32)] + [shape(chunk, BF16)] * (n - 1),
        [
            pltpu.VMEM((2 * HALO * ny, nz, ch), F32),
            pltpu.VMEM((4, HALO, n * ny + 2, nz, ch), BF16),
            pltpu.VMEM((3, half_y + 2, half_x + 2, half_z, width), F32),
            pltpu.VMEM((n,) + chunk, F32),
            pltpu.VMEM(filters_half.shape, BF16),
            pltpu.SemaphoreType.DMA((3,)),
        ],
        (*rims, inner, full, up, filters_half),
        far=1,
    )
    parts = [chunks[0]]
    for k in range(1, n):
        parts.append(swap(chunks[k], "chan", k))
    (grad_half,) = call(sum_kernel, [shape(chunk, BF16)], [], parts, False)
    for bit in range(1, m.bit_length() - 1):
        rows = keep.shape[0] // 2
        keep, send = call(
            lambda *refs: fold_kernel(bit, *refs),
            [shape((rows, lanes), F32), shape((rows, lanes), BF16)],
            [],
            (keep, got) if bit > 1 else (keep, got, outer),
        )
        got = swap(send, "grp", 2**bit)
    (taps_grad,) = call(
        finish_kernel, [shape((3, 3, 3, ch // m, ch // n), F32)], [], (keep, got), False
    )
    return (grad_half, taps_grad)


def solution(mesh):
    in_specs = (
        P("grp", "chan", None, None),
        P("grp", "chan", None, None),
        P(),
        P(),
        P(None, None, None, None, "chan"),
    )
    out_specs = (P("chan", "grp", None, None), P(None, None, None, "grp", "chan"))
    return jax.shard_map(work, mesh=mesh, in_specs=in_specs, out_specs=out_specs, check_vma=False)
```

```python
import jax
import jax.numpy as jnp
from jax import lax
from jax.experimental import pallas as pl
from jax.experimental.pallas import tpu as pltpu
from jax.sharding import PartitionSpec as P


F32 = jnp.float32
BF16 = jnp.bfloat16
LIMIT = 20 * 2**20
HALO = 3
NT = (((1,), (1,)), ((), ()))
NN = (((1,), (0,)), ((), ()))


def dot(a, b, dims):
    return lax.dot_general(a, b, dims, preferred_element_type=F32)


def swap(value, axis, k):
    n = lax.axis_size(axis)
    return lax.ppermute(value, axis, [(i, i ^ k) for i in range(n)])


def shift(value, axis, step):
    n = lax.axis_size(axis)
    return lax.ppermute(value, axis, [(i, (i + step) % n) for i in range(n)])


def pair(k):
    return jnp.bitwise_xor(lax.axis_index("chan"), k)


def fetch_kernel(*refs):
    count = len(refs) // 2
    arrived = refs[2 * count]
    copies = []
    for k in range(count):
        source, target = refs[k], refs[count + k]
        if source.shape != target.shape:
            width = target.shape[3]
            start = pl.multiple_of(lax.axis_index("chan") * width, width)
            source = source.at[:, :, :, pl.ds(start, width), :]
        copies.append(pltpu.make_async_copy(source, target, arrived.at[k]))
    for copy in copies:
        copy.start()
    for copy in copies:
        copy.wait()


def spread_out(sources, full_ref, stage, spread):
    ny, nz, ch = sources[0][0].shape[1:]
    count = sum(source.shape[0] for source in sources[0])
    n, pairs, half_z = len(sources), count // 2, nz // 2
    rows = n * ny
    spread[:, :, 0] = jnp.zeros((4, pairs, nz, ch), BF16)
    spread[:, :, rows + 1] = jnp.zeros((4, pairs, nz, ch), BF16)
    level = lax.broadcasted_iota(jnp.int32, (count * ny, half_z, ch), 1)
    for k in range(n):
        at = 0
        for source in sources[k]:
            size = source.shape[0] * ny
            stage[at : at + size] = source.astype(F32).reshape(size, nz, ch)
            at += size
        even = stage[:, pl.ds(0, half_z, stride=2), :]
        odd = stage[:, pl.ds(1, half_z, stride=2), :]
        after = jnp.where(level == half_z - 1, 0.0, pltpu.roll(even, half_z - 1, 1))
        before = jnp.where(level == 0, 0.0, pltpu.roll(odd, 1, 1))
        first = pair(k) * ny + 1
        for which, value in enumerate((even, after, odd, before)):
            value = value.reshape(pairs, 2, ny, half_z, ch)
            for b in range(ny):
                packed = jnp.concatenate([value[:, 0, b], value[:, 1, b]], axis=1)
                spread[which, :, first + b] = packed.astype(BF16)
    taps = jnp.concatenate(
        [
            jnp.concatenate([full_ref[p, q, r] for q in range(3) for r in range(3)], axis=1)
            for p in range(3)
        ],
        axis=0,
    )
    products = []
    for order in ((2, 0, 3), (1, 2, 0)):
        window = jnp.concatenate(
            [
                spread[which, :, 2 - q : 2 - q + rows].reshape(pairs * rows * nz, ch)
                for q in range(3)
                for which in order
            ],
            axis=1,
        )
        products.append(dot(window, taps, NT).reshape(pairs, rows, 2, half_z, 3 * ch))
    return products


def inner_kernel(n, *refs):
    bricks, (full_ref, out_ref, stage, spread) = refs[:n], refs[n:]
    nx, ch = bricks[0].shape[0] // 2, bricks[0].shape[3]
    products = spread_out([[brick[:nx]] for brick in bricks], full_ref, stage, spread)
    for c, product in enumerate(products):
        for u in range(-1, nx + 1):
            total = None
            for p in range(3):
                x = u - p + 1
                if 0 <= x < nx:
                    term = product[x // 2, :, x % 2, :, p * ch : (p + 1) * ch]
                    total = term if total is None else total + term
            out_ref[c, u + 1] = total


def main_kernel(n, m, *refs):
    rims, (inner_ref, full_ref, up_ref, half_ref) = refs[:n], refs[n : n + 4]
    outs, (stage, spread, padded, result, held, arrived) = refs[n + 4 : n + 6], refs[n + 6 :]
    loads = [
        pltpu.make_async_copy(half_ref.at[p], held.at[p], arrived.at[p]) for p in range(3)
    ]
    for load in loads:
        load.start()
    halo = rims[0].shape[0] // 2 - 1
    nx, rows, half_z, ch = inner_ref.shape[1:]
    nx = nx - 2
    half_x, half_y = nx // 2, rows // 2
    width = up_ref.shape[3]
    products = spread_out([[rim[: 2 * halo]] for rim in rims], full_ref, stage, spread)
    grads = []
    for c, product in enumerate(products):
        planes = {}
        for u in range(-2, nx + 2):
            total = inner_ref[c, u + 1] if -1 <= u <= nx else None
            for p in range(3):
                x = u - p + 1
                if not 0 <= x < nx:
                    at = x + halo if x < 0 else x - nx + halo
                    term = product[at // 2, :, at % 2, :, p * ch : (p + 1) * ch]
                    total = term if total is None else total + term
            planes[u] = total.reshape(half_y, 2, half_z, ch)
        grads.append(planes)
    columns = []
    for a in range(2):
        for b in range(2):
            for c in range(2):
                pieces = [
                    grads[c][2 * i + a][:, b].reshape(half_y * half_z, ch)
                    for i in range(-1, half_x + 1)
                ]
                columns.append(jnp.concatenate(pieces, axis=0).astype(BF16))
    up = jnp.concatenate(
        [up_ref[a, b, c] for a in range(2) for b in range(2) for c in range(2)], axis=1
    )
    wide_x = half_x + 2
    coarse = dot(jnp.concatenate(columns, axis=1), up, NT).reshape(wide_x, half_y, half_z, width)
    g = lax.axis_index("grp")
    low = jnp.where(g > 0, 1.0, 0.0)
    high = jnp.where(g < m - 1, 1.0, 0.0)
    padded[:, 0] = jnp.zeros((3, wide_x, half_z, width), F32)
    padded[:, half_y + 1] = jnp.zeros((3, wide_x, half_z, width), F32)
    level = lax.broadcasted_iota(jnp.int32, (half_y, half_z, width), 1)
    for i in range(wide_x):
        plane = coarse[i]
        if i == 0:
            plane = plane * low
        if i == wide_x - 1:
            plane = plane * high
        plane = plane.astype(BF16).astype(F32)
        padded[0, 1 : half_y + 1, i] = jnp.where(
            level == half_z - 1, 0.0, pltpu.roll(plane, half_z - 1, 1)
        )
        padded[1, 1 : half_y + 1, i] = plane
        padded[2, 1 : half_y + 1, i] = jnp.where(level == 0, 0.0, pltpu.roll(plane, 1, 1))
    cells = half_y * half_x * half_z
    total = None
    for p in range(3):
        loads[p].wait()
        windows = [
            padded[r, 2 - q : 2 - q + half_y, 2 - p : 2 - p + half_x]
            .reshape(cells, width)
            .astype(BF16)
            for q in range(3)
            for r in range(3)
        ]
        kernels = [held[p, q, r] for q in range(3) for r in range(3)]
        if width % 128 == 0:
            windows = [jnp.concatenate(windows, axis=1)]
            kernels = [jnp.concatenate(kernels, axis=1)]
        for window, kernel in zip(windows, kernels):
            product = dot(window, kernel, NT)
            total = product if total is None else total + product
    result[...] = total.reshape(result.shape)
    for k in range(n):
        out = outs[k // (n // 2)]
        out[k % (n // 2)] = result[pair(k)].astype(out.dtype)


def chosen_lanes(cells, pick, part, nz):
    chosen = dot(cells, pick, NN)
    level = lax.rem(lax.broadcasted_iota(jnp.int32, chosen.shape, 0), nz)
    lane = lax.broadcasted_iota(jnp.int32, chosen.shape, 1)
    count = chosen.shape[0]
    above = jnp.where(level == nz - 1, 0.0, pltpu.roll(chosen, count - 1, 0))
    below = jnp.where(level == 0, 0.0, pltpu.roll(chosen, 1, 0))
    mixed = jnp.where(lane < part, above, jnp.where(lane < 2 * part, chosen, below))
    return mixed.astype(BF16)


def selections(n, m, ch):
    part, block = ch // n, ch // m
    start = lax.axis_index("chan") * part
    source = lax.broadcasted_iota(jnp.int32, (ch, ch), 0)
    target = lax.broadcasted_iota(jnp.int32, (ch, ch), 1)
    copies = (lax.rem(target, part) + start == source) & (target < 3 * part)
    pick = jnp.where(copies, 1.0, 0.0).astype(BF16)
    bits = m.bit_length() - 1
    owner = target // block
    turned = jnp.zeros_like(owner)
    for bit in range(bits):
        turned = turned + (owner // 2**bit % 2) * 2 ** (bits - 1 - bit)
    place = turned * block + lax.rem(target, block)
    return pick, place, source


def taps_kernel(n, m, *refs):
    bricks, (keep_ref, send_ref, spread, table) = refs[:n], refs[n:]
    nx, ny, nz, ch = bricks[0].shape
    nx = nx // 2
    rows = n * ny
    part = ch // n
    cells = nx * ny * nz
    spread[:, 0] = jnp.zeros((nx, nz, ch), BF16)
    spread[:, rows + 1] = jnp.zeros((nx, nz, ch), BF16)
    pick, place, source = selections(n, m, ch)
    order = jnp.where(place == source, 1.0, 0.0).astype(BF16)
    turned_feats = []
    for k in range(n):
        mixed = chosen_lanes(bricks[k][:nx].reshape(cells, ch), pick, part, nz)
        mixed = mixed.reshape(nx, ny, nz, ch)
        first = pair(k) * ny + 1
        for b in range(ny):
            spread[:, first + b] = mixed[:, b]
        turned_feats.append(dot(order, bricks[k][nx:].reshape(cells, ch), NT).astype(BF16))
    totals = []
    plane = ny * nz
    for p in range(3):
        total = None
        feat_from, grad_from = max(0, p - 1), max(0, 1 - p)
        count = nx - abs(p - 1)
        for k in range(n):
            first = pair(k) * ny
            window = jnp.concatenate(
                [
                    spread[
                        grad_from : grad_from + count, pl.ds(first + 2 - q, ny)
                    ].reshape(count * plane, ch)
                    for q in range(3)
                ],
                axis=1,
            )
            feat = turned_feats[k][:, feat_from * plane : (feat_from + count) * plane]
            product = dot(feat, window, NN)
            total = product if total is None else total + product
        totals += [total[:, q * ch : q * ch + 3 * part] for q in range(3)]
    table[...] = jnp.concatenate(totals, axis=1)
    half = ch // 2
    bit = lax.rem(lax.axis_index("grp"), 2)
    keep_ref[...] = table[pl.ds(pl.multiple_of(bit * half, half), half), :]
    send_ref[...] = table[pl.ds(pl.multiple_of((1 - bit) * half, half), half), :].astype(BF16)


def outer_kernel(n, m, *refs):
    bricks, rims, (out_ref, spread) = refs[:n], refs[n : 2 * n], refs[2 * n :]
    nx, ny, nz, ch = bricks[0].shape
    nx = nx // 2
    halo = rims[0].shape[0] // 2 - 1
    rows = n * ny
    part = ch // n
    plane = ny * nz
    half = ch // 2
    spread[:, 0] = jnp.zeros((4, nz, ch), BF16)
    spread[:, rows + 1] = jnp.zeros((4, nz, ch), BF16)
    pick, place, source = selections(n, m, ch)
    bit = lax.rem(lax.axis_index("grp"), 2)
    order = jnp.where(place[:half] == source[:half] + bit * half, 1.0, 0.0).astype(BF16)
    cells = []
    for k in range(n):
        for planes in (
            bricks[k][0:1],
            rims[k][halo : halo + 1],
            rims[k][halo - 1 : halo],
            bricks[k][nx - 1 : nx],
        ):
            cells.append(planes.reshape(plane, ch))
    mixed = chosen_lanes(jnp.concatenate(cells, axis=0), pick, part, nz)
    mixed = mixed.reshape(n, 4, ny, nz, ch)
    for k in range(n):
        first = pair(k) * ny + 1
        for b in range(ny):
            spread[:, first + b] = mixed[k, :, b]
    for e in range(2):
        feats, windows = [], []
        for k in range(n):
            if e == 0:
                sides = (rims[k][2 * halo], bricks[k][2 * nx - 1])
            else:
                sides = (bricks[k][nx], rims[k][2 * halo + 1])
            first = pair(k) * ny
            for side, feat in enumerate(sides):
                feats.append(feat.reshape(plane, ch))
                windows.append(
                    jnp.concatenate(
                        [
                            spread[2 * e + side, pl.ds(first + 2 - q, ny)].reshape(plane, ch)
                            for q in range(3)
                        ],
                        axis=1,
                    )
                )
        feat = dot(order, jnp.concatenate(feats, axis=0), NT).astype(BF16)
        total = dot(feat, jnp.concatenate(windows, axis=0), NN)
        out_ref[e] = jnp.concatenate(
            [total[:, q * ch : q * ch + 3 * part] for q in range(3)], axis=1
        )


def load_kernel(grad_ref, feat_ref, own_ref, first_ref, last_ref, arrived):
    nx = grad_ref.shape[0]
    halo = first_ref.shape[0] - 1
    cut = pl.ds(0, halo)
    copies = [
        pltpu.make_async_copy(
            grad_ref.at[pl.ds(nx - halo, halo)], last_ref.at[cut], arrived.at[0]
        ),
        pltpu.make_async_copy(grad_ref.at[cut], first_ref.at[cut], arrived.at[1]),
        pltpu.make_async_copy(feat_ref.at[nx - 1], last_ref.at[halo], arrived.at[4]),
        pltpu.make_async_copy(feat_ref.at[0], first_ref.at[halo], arrived.at[5]),
        pltpu.make_async_copy(grad_ref, own_ref.at[pl.ds(0, nx)], arrived.at[2]),
        pltpu.make_async_copy(feat_ref, own_ref.at[pl.ds(nx, nx)], arrived.at[3]),
    ]
    for copy in copies:
        copy.start()
    for copy in copies:
        copy.wait()


def rims_kernel(m, left_ref, right_ref, out_ref):
    g = lax.axis_index("grp")
    halo = left_ref.shape[0] - 1
    left, right = left_ref[...], right_ref[...]
    left = jnp.where(g > 0, left, jnp.zeros_like(left))
    right = jnp.where(g < m - 1, right, jnp.zeros_like(right))
    out_ref[:halo] = left[:halo]
    out_ref[halo : 2 * halo] = right[:halo]
    out_ref[2 * halo] = left[halo]
    out_ref[2 * halo + 1] = right[halo]


def fold_kernel(bit, keep_ref, got_ref, *refs):
    extra, (held_ref, send_ref) = refs[:-2], refs[-2:]
    total = keep_ref[...] + got_ref[...].astype(F32)
    if extra:
        (outer_ref,) = extra
        third = outer_ref.shape[2]
        total = jnp.concatenate(
            [
                total[:, :third] + outer_ref[0],
                total[:, third : 2 * third],
                total[:, 2 * third :] + outer_ref[1],
            ],
            axis=1,
        )
    half = held_ref.shape[0]
    upper = lax.rem(lax.axis_index("grp") // 2**bit, 2) == 1
    held_ref[...] = jnp.where(upper, total[half:], total[:half])
    send_ref[...] = jnp.where(upper, total[:half], total[half:]).astype(BF16)


def finish_kernel(keep_ref, got_ref, out_ref):
    part = out_ref.shape[4]
    total = keep_ref[...] + got_ref[...].astype(F32)
    for p in range(3):
        for q in range(3):
            for r in range(3):
                at = (9 * p + 3 * q + r) * part
                out_ref[p, q, r] = total[:, at : at + part]


def halve_kernel(keep_ref, got_ref, held_ref, send_ref):
    half = held_ref.shape[0]
    held_ref[...] = keep_ref[:half] + got_ref[:half].astype(F32)
    send_ref[...] = (keep_ref[half:] + got_ref[half:].astype(F32)).astype(BF16)


def sum_kernel(keep_ref, got_ref, out_ref):
    out_ref[...] = (keep_ref[0] + got_ref[0].astype(F32)).astype(BF16)


def call(kernel, outs, scratch, inputs, placed=True, far=0):
    spaces = [pltpu.VMEM] * (len(inputs) - far) + [pltpu.HBM] * far
    return pl.pallas_call(
        kernel,
        out_shape=[pltpu.VMEM(v.shape, v.dtype) if placed else v for v in outs],
        in_specs=[pl.BlockSpec(memory_space=space) for space in spaces],
        out_specs=[pl.BlockSpec(memory_space=pltpu.VMEM)] * len(outs),
        scratch_shapes=scratch,
        compiler_params=pltpu.CompilerParams(vmem_limit_bytes=LIMIT),
    )(*[pltpu.with_memory_space_constraint(v, space) for v, space in zip(inputs, spaces)])


def fetch(weights, shapes):
    count = len(weights)
    return pl.pallas_call(
        fetch_kernel,
        out_shape=[pltpu.VMEM(shape, BF16) for shape in shapes],
        in_specs=[pl.BlockSpec(memory_space=pltpu.HBM)] * count,
        out_specs=[pl.BlockSpec(memory_space=pltpu.VMEM)] * count,
        scratch_shapes=[pltpu.SemaphoreType.DMA((count,))],
        compiler_params=pltpu.CompilerParams(vmem_limit_bytes=LIMIT),
    )(*[pltpu.with_memory_space_constraint(v, pltpu.HBM) for v in weights])


def gather(value):
    held = {0: value}
    k = lax.axis_size("chan") // 2
    while k:
        for j in list(held):
            held[j ^ k] = swap(held[j], "chan", k)
        k //= 2
    return [held[j] for j in sorted(held)]


def work(grad_out, feat_full, filters_full, upsample_weight, filters_half):
    n, m = lax.axis_size("chan"), lax.axis_size("grp")
    nx, ny, nz, ch = grad_out.shape
    half_x, half_y, half_z = nx // 2, n * ny // 2, nz // 2
    width = filters_half.shape[4]
    lanes = 27 * (ch // n)
    shape = jax.ShapeDtypeStruct
    edge = shape((HALO + 1, ny, nz, ch), BF16)
    own, first, last = call(
        load_kernel,
        [shape((2 * nx, ny, nz, ch), BF16), edge, edge],
        [pltpu.SemaphoreType.DMA((6,))],
        (grad_out, feat_full),
        far=2,
    )
    from_left = shift(last, "grp", 1)
    from_right = shift(first, "grp", -1)
    bricks = gather(own)
    (rim,) = call(
        lambda *refs: rims_kernel(m, *refs),
        [shape((2 * HALO + 2, ny, nz, ch), BF16)],
        [],
        (from_left, from_right),
    )
    rims = gather(rim)
    up = upsample_weight.shape[:3] + (width, ch)
    full, up = fetch((filters_full, upsample_weight), (filters_full.shape, up))
    keep, send = call(
        lambda *refs: taps_kernel(n, m, *refs),
        [shape((ch // 2, lanes), F32), shape((ch // 2, lanes), BF16)],
        [pltpu.VMEM((nx, n * ny + 2, nz, ch), BF16), pltpu.VMEM((ch, lanes), F32)],
        tuple(bricks),
    )
    (outer,) = call(
        lambda *refs: outer_kernel(n, m, *refs),
        [shape((2, ch // 2, lanes // 3), F32)],
        [pltpu.VMEM((4, n * ny + 2, nz, ch), BF16)],
        (*bricks, *rims),
    )
    got = swap(send, "grp", 1)
    (inner,) = call(
        lambda *refs: inner_kernel(n, *refs),
        [shape((2, nx + 2, n * ny, half_z, ch), F32)],
        [
            pltpu.VMEM((nx * ny, nz, ch), F32),
            pltpu.VMEM((4, half_x, n * ny + 2, nz, ch), BF16),
        ],
        (*bricks, full),
    )
    chunk = (half_y // n, half_x, half_z, filters_half.shape[3])
    own_sum, other = call(
        lambda *refs: main_kernel(n, m, *refs),
        [shape((n // 2,) + chunk, F32), shape((n // 2,) + chunk, BF16)],
        [
            pltpu.VMEM((2 * HALO * ny, nz, ch), F32),
            pltpu.VMEM((4, HALO, n * ny + 2, nz, ch), BF16),
            pltpu.VMEM((3, half_y + 2, half_x + 2, half_z, width), F32),
            pltpu.VMEM((n,) + chunk, F32),
            pltpu.VMEM(filters_half.shape, BF16),
            pltpu.SemaphoreType.DMA((3,)),
        ],
        (*rims, inner, full, up, filters_half),
        far=1,
    )
    got_sum = swap(other, "chan", n // 2)
    for bit in range(1, n.bit_length() - 1):
        count = own_sum.shape[0] // 2
        own_sum, other = call(
            halve_kernel,
            [shape((count,) + chunk, F32), shape((count,) + chunk, BF16)],
            [],
            (own_sum, got_sum),
        )
        got_sum = swap(other, "chan", n // 2 ** (bit + 1))
    (grad_half,) = call(sum_kernel, [shape(chunk, BF16)], [], (own_sum, got_sum), False)
    for bit in range(1, m.bit_length() - 1):
        rows = keep.shape[0] // 2
        keep, send = call(
            lambda *refs: fold_kernel(bit, *refs),
            [shape((rows, lanes), F32), shape((rows, lanes), BF16)],
            [],
            (keep, got) if bit > 1 else (keep, got, outer),
        )
        got = swap(send, "grp", 2**bit)
    (taps_grad,) = call(
        finish_kernel, [shape((3, 3, 3, ch // m, ch // n), F32)], [], (keep, got), False
    )
    return (grad_half, taps_grad)


def solution(mesh):
    in_specs = (
        P("grp", "chan", None, None),
        P("grp", "chan", None, None),
        P(),
        P(),
        P(None, None, None, None, "chan"),
    )
    out_specs = (P("chan", "grp", None, None), P(None, None, None, "grp", "chan"))
    return jax.shard_map(work, mesh=mesh, in_specs=in_specs, out_specs=out_specs, check_vma=False)
```

```python
import jax
import jax.numpy as jnp
from jax import lax
from jax.experimental import pallas as pl
from jax.experimental.pallas import tpu as pltpu
from jax.sharding import PartitionSpec as P


F32 = jnp.float32
BF16 = jnp.bfloat16
LIMIT = 20 * 2**20
HALO = 3
NT = (((1,), (1,)), ((), ()))
NN = (((1,), (0,)), ((), ()))


def dot(a, b, dims):
    return lax.dot_general(a, b, dims, preferred_element_type=F32)


def swap(value, axis, k):
    n = lax.axis_size(axis)
    return lax.ppermute(value, axis, [(i, i ^ k) for i in range(n)])


def shift(value, axis, step):
    n = lax.axis_size(axis)
    return lax.ppermute(value, axis, [(i, (i + step) % n) for i in range(n)])


def pair(k):
    return jnp.bitwise_xor(lax.axis_index("chan"), k)


def fetch_kernel(*refs):
    count = len(refs) // 2
    arrived = refs[2 * count]
    copies = []
    for k in range(count):
        source, target = refs[k], refs[count + k]
        if source.shape != target.shape:
            width = target.shape[3]
            start = pl.multiple_of(lax.axis_index("chan") * width, width)
            source = source.at[:, :, :, pl.ds(start, width), :]
        copies.append(pltpu.make_async_copy(source, target, arrived.at[k]))
    for copy in copies:
        copy.start()
    for copy in copies:
        copy.wait()


def spread_out(sources, full_ref, stage, spread):
    ny, nz, ch = sources[0][0].shape[1:]
    count = sum(source.shape[0] for source in sources[0])
    n, pairs, half_z = len(sources), count // 2, nz // 2
    rows = n * ny
    spread[:, :, 0] = jnp.zeros((4, pairs, nz, ch), BF16)
    spread[:, :, rows + 1] = jnp.zeros((4, pairs, nz, ch), BF16)
    level = lax.broadcasted_iota(jnp.int32, (count * ny, half_z, ch), 1)
    for k in range(n):
        at = 0
        for source in sources[k]:
            size = source.shape[0] * ny
            stage[at : at + size] = source.astype(F32).reshape(size, nz, ch)
            at += size
        even = stage[:, pl.ds(0, half_z, stride=2), :]
        odd = stage[:, pl.ds(1, half_z, stride=2), :]
        after = jnp.where(level == half_z - 1, 0.0, pltpu.roll(even, half_z - 1, 1))
        before = jnp.where(level == 0, 0.0, pltpu.roll(odd, 1, 1))
        first = pair(k) * ny + 1
        for which, value in enumerate((even, after, odd, before)):
            value = value.reshape(pairs, 2, ny, half_z, ch)
            for b in range(ny):
                packed = jnp.concatenate([value[:, 0, b], value[:, 1, b]], axis=1)
                spread[which, :, first + b] = packed.astype(BF16)
    taps = jnp.concatenate(
        [
            jnp.concatenate([full_ref[p, q, r] for q in range(3) for r in range(3)], axis=1)
            for p in range(3)
        ],
        axis=0,
    )
    products = []
    for order in ((2, 0, 3), (1, 2, 0)):
        window = jnp.concatenate(
            [
                spread[which, :, 2 - q : 2 - q + rows].reshape(pairs * rows * nz, ch)
                for q in range(3)
                for which in order
            ],
            axis=1,
        )
        products.append(dot(window, taps, NT).reshape(pairs, rows, 2, half_z, 3 * ch))
    return products


def inner_kernel(n, *refs):
    bricks, (full_ref, out_ref, stage, spread) = refs[:n], refs[n:]
    nx, ch = bricks[0].shape[0] // 2, bricks[0].shape[3]
    products = spread_out([[brick[:nx]] for brick in bricks], full_ref, stage, spread)
    for c, product in enumerate(products):
        for u in range(-1, nx + 1):
            total = None
            for p in range(3):
                x = u - p + 1
                if 0 <= x < nx:
                    term = product[x // 2, :, x % 2, :, p * ch : (p + 1) * ch]
                    total = term if total is None else total + term
            out_ref[c, u + 1] = total


def main_kernel(n, m, *refs):
    rims, (inner_ref, full_ref, up_ref, half_ref) = refs[:n], refs[n : n + 4]
    outs, (stage, spread, padded, result, held, arrived) = (
        refs[n + 4 : 2 * n + 4],
        refs[2 * n + 4 :],
    )
    loads = [
        pltpu.make_async_copy(half_ref.at[p], held.at[p], arrived.at[p]) for p in range(3)
    ]
    for load in loads:
        load.start()
    halo = rims[0].shape[0] // 2 - 1
    nx, rows, half_z, ch = inner_ref.shape[1:]
    nx = nx - 2
    half_x, half_y = nx // 2, rows // 2
    width = up_ref.shape[3]
    products = spread_out([[rim[: 2 * halo]] for rim in rims], full_ref, stage, spread)
    grads = []
    for c, product in enumerate(products):
        planes = {}
        for u in range(-2, nx + 2):
            total = inner_ref[c, u + 1] if -1 <= u <= nx else None
            for p in range(3):
                x = u - p + 1
                if not 0 <= x < nx:
                    at = x + halo if x < 0 else x - nx + halo
                    term = product[at // 2, :, at % 2, :, p * ch : (p + 1) * ch]
                    total = term if total is None else total + term
            planes[u] = total.reshape(half_y, 2, half_z, ch)
        grads.append(planes)
    columns = []
    for a in range(2):
        for b in range(2):
            for c in range(2):
                pieces = [
                    grads[c][2 * i + a][:, b].reshape(half_y * half_z, ch)
                    for i in range(-1, half_x + 1)
                ]
                columns.append(jnp.concatenate(pieces, axis=0).astype(BF16))
    up = jnp.concatenate(
        [up_ref[a, b, c] for a in range(2) for b in range(2) for c in range(2)], axis=1
    )
    wide_x = half_x + 2
    coarse = dot(jnp.concatenate(columns, axis=1), up, NT).reshape(wide_x, half_y, half_z, width)
    g = lax.axis_index("grp")
    low = jnp.where(g > 0, 1.0, 0.0)
    high = jnp.where(g < m - 1, 1.0, 0.0)
    padded[:, 0] = jnp.zeros((3, wide_x, half_z, width), F32)
    padded[:, half_y + 1] = jnp.zeros((3, wide_x, half_z, width), F32)
    level = lax.broadcasted_iota(jnp.int32, (half_y, half_z, width), 1)
    for i in range(wide_x):
        plane = coarse[i]
        if i == 0:
            plane = plane * low
        if i == wide_x - 1:
            plane = plane * high
        plane = plane.astype(BF16).astype(F32)
        padded[0, 1 : half_y + 1, i] = jnp.where(
            level == half_z - 1, 0.0, pltpu.roll(plane, half_z - 1, 1)
        )
        padded[1, 1 : half_y + 1, i] = plane
        padded[2, 1 : half_y + 1, i] = jnp.where(level == 0, 0.0, pltpu.roll(plane, 1, 1))
    cells = half_y * half_x * half_z
    total = None
    for p in range(3):
        loads[p].wait()
        windows = [
            padded[r, 2 - q : 2 - q + half_y, 2 - p : 2 - p + half_x]
            .reshape(cells, width)
            .astype(BF16)
            for q in range(3)
            for r in range(3)
        ]
        kernels = [held[p, q, r] for q in range(3) for r in range(3)]
        if width % 128 == 0:
            windows = [jnp.concatenate(windows, axis=1)]
            kernels = [jnp.concatenate(kernels, axis=1)]
        for window, kernel in zip(windows, kernels):
            product = dot(window, kernel, NT)
            total = product if total is None else total + product
    result[...] = total.reshape(result.shape)
    for k in range(n):
        outs[k][...] = result[pair(k)].astype(outs[k].dtype)


def chosen_lanes(cells, pick, part, nz):
    chosen = dot(cells, pick, NN)
    level = lax.rem(lax.broadcasted_iota(jnp.int32, chosen.shape, 0), nz)
    lane = lax.broadcasted_iota(jnp.int32, chosen.shape, 1)
    count = chosen.shape[0]
    above = jnp.where(level == nz - 1, 0.0, pltpu.roll(chosen, count - 1, 0))
    below = jnp.where(level == 0, 0.0, pltpu.roll(chosen, 1, 0))
    mixed = jnp.where(lane < part, above, jnp.where(lane < 2 * part, chosen, below))
    return mixed.astype(BF16)


def selections(n, m, ch):
    part, block = ch // n, ch // m
    start = lax.axis_index("chan") * part
    source = lax.broadcasted_iota(jnp.int32, (ch, ch), 0)
    target = lax.broadcasted_iota(jnp.int32, (ch, ch), 1)
    copies = (lax.rem(target, part) + start == source) & (target < 3 * part)
    pick = jnp.where(copies, 1.0, 0.0).astype(BF16)
    bits = m.bit_length() - 1
    owner = target // block
    turned = jnp.zeros_like(owner)
    for bit in range(bits):
        turned = turned + (owner // 2**bit % 2) * 2 ** (bits - 1 - bit)
    place = turned * block + lax.rem(target, block)
    return pick, place, source


def taps_kernel(n, m, *refs):
    bricks, (keep_ref, send_ref, spread, table) = refs[:n], refs[n:]
    nx, ny, nz, ch = bricks[0].shape
    nx = nx // 2
    rows = n * ny
    part = ch // n
    cells = nx * ny * nz
    spread[:, 0] = jnp.zeros((nx, nz, ch), BF16)
    spread[:, rows + 1] = jnp.zeros((nx, nz, ch), BF16)
    pick, place, source = selections(n, m, ch)
    order = jnp.where(place == source, 1.0, 0.0).astype(BF16)
    turned_feats = []
    for k in range(n):
        mixed = chosen_lanes(bricks[k][:nx].reshape(cells, ch), pick, part, nz)
        mixed = mixed.reshape(nx, ny, nz, ch)
        first = pair(k) * ny + 1
        for b in range(ny):
            spread[:, first + b] = mixed[:, b]
        turned_feats.append(dot(order, bricks[k][nx:].reshape(cells, ch), NT).astype(BF16))
    totals = []
    plane = ny * nz
    for p in range(3):
        total = None
        feat_from, grad_from = max(0, p - 1), max(0, 1 - p)
        count = nx - abs(p - 1)
        for k in range(n):
            first = pair(k) * ny
            window = jnp.concatenate(
                [
                    spread[
                        grad_from : grad_from + count, pl.ds(first + 2 - q, ny)
                    ].reshape(count * plane, ch)
                    for q in range(3)
                ],
                axis=1,
            )
            feat = turned_feats[k][:, feat_from * plane : (feat_from + count) * plane]
            product = dot(feat, window, NN)
            total = product if total is None else total + product
        totals += [total[:, q * ch : q * ch + 3 * part] for q in range(3)]
    table[...] = jnp.concatenate(totals, axis=1)
    half = ch // 2
    bit = lax.rem(lax.axis_index("grp"), 2)
    keep_ref[...] = table[pl.ds(pl.multiple_of(bit * half, half), half), :]
    send_ref[...] = table[pl.ds(pl.multiple_of((1 - bit) * half, half), half), :].astype(BF16)


def outer_kernel(n, m, *refs):
    bricks, rims, (out_ref, spread) = refs[:n], refs[n : 2 * n], refs[2 * n :]
    nx, ny, nz, ch = bricks[0].shape
    nx = nx // 2
    halo = rims[0].shape[0] // 2 - 1
    rows = n * ny
    part = ch // n
    plane = ny * nz
    half = ch // 2
    spread[:, 0] = jnp.zeros((4, nz, ch), BF16)
    spread[:, rows + 1] = jnp.zeros((4, nz, ch), BF16)
    pick, place, source = selections(n, m, ch)
    bit = lax.rem(lax.axis_index("grp"), 2)
    order = jnp.where(place[:half] == source[:half] + bit * half, 1.0, 0.0).astype(BF16)
    cells = []
    for k in range(n):
        for planes in (
            bricks[k][0:1],
            rims[k][halo : halo + 1],
            rims[k][halo - 1 : halo],
            bricks[k][nx - 1 : nx],
        ):
            cells.append(planes.reshape(plane, ch))
    mixed = chosen_lanes(jnp.concatenate(cells, axis=0), pick, part, nz)
    mixed = mixed.reshape(n, 4, ny, nz, ch)
    for k in range(n):
        first = pair(k) * ny + 1
        for b in range(ny):
            spread[:, first + b] = mixed[k, :, b]
    for e in range(2):
        feats, windows = [], []
        for k in range(n):
            if e == 0:
                sides = (rims[k][2 * halo], bricks[k][2 * nx - 1])
            else:
                sides = (bricks[k][nx], rims[k][2 * halo + 1])
            first = pair(k) * ny
            for side, feat in enumerate(sides):
                feats.append(feat.reshape(plane, ch))
                windows.append(
                    jnp.concatenate(
                        [
                            spread[2 * e + side, pl.ds(first + 2 - q, ny)].reshape(plane, ch)
                            for q in range(3)
                        ],
                        axis=1,
                    )
                )
        feat = dot(order, jnp.concatenate(feats, axis=0), NT).astype(BF16)
        total = dot(feat, jnp.concatenate(windows, axis=0), NN)
        out_ref[e] = jnp.concatenate(
            [total[:, q * ch : q * ch + 3 * part] for q in range(3)], axis=1
        )


def load_kernel(grad_ref, feat_ref, own_ref, first_ref, last_ref, arrived):
    nx = grad_ref.shape[0]
    halo = first_ref.shape[0] - 1
    cut = pl.ds(0, halo)
    copies = [
        pltpu.make_async_copy(
            grad_ref.at[pl.ds(nx - halo, halo)], last_ref.at[cut], arrived.at[0]
        ),
        pltpu.make_async_copy(grad_ref.at[cut], first_ref.at[cut], arrived.at[1]),
        pltpu.make_async_copy(feat_ref.at[nx - 1], last_ref.at[halo], arrived.at[4]),
        pltpu.make_async_copy(feat_ref.at[0], first_ref.at[halo], arrived.at[5]),
        pltpu.make_async_copy(grad_ref, own_ref.at[pl.ds(0, nx)], arrived.at[2]),
        pltpu.make_async_copy(feat_ref, own_ref.at[pl.ds(nx, nx)], arrived.at[3]),
    ]
    for copy in copies:
        copy.start()
    for copy in copies:
        copy.wait()


def rims_kernel(m, left_ref, right_ref, out_ref):
    g = lax.axis_index("grp")
    halo = left_ref.shape[0] - 1
    left, right = left_ref[...], right_ref[...]
    left = jnp.where(g > 0, left, jnp.zeros_like(left))
    right = jnp.where(g < m - 1, right, jnp.zeros_like(right))
    out_ref[:halo] = left[:halo]
    out_ref[halo : 2 * halo] = right[:halo]
    out_ref[2 * halo] = left[halo]
    out_ref[2 * halo + 1] = right[halo]


def fold_kernel(bit, keep_ref, got_ref, *refs):
    extra, (held_ref, send_ref) = refs[:-2], refs[-2:]
    total = keep_ref[...] + got_ref[...].astype(F32)
    if extra:
        (outer_ref,) = extra
        third = outer_ref.shape[2]
        total = jnp.concatenate(
            [
                total[:, :third] + outer_ref[0],
                total[:, third : 2 * third],
                total[:, 2 * third :] + outer_ref[1],
            ],
            axis=1,
        )
    half = held_ref.shape[0]
    upper = lax.rem(lax.axis_index("grp") // 2**bit, 2) == 1
    held_ref[...] = jnp.where(upper, total[half:], total[:half])
    send_ref[...] = jnp.where(upper, total[:half], total[half:]).astype(BF16)


def finish_kernel(keep_ref, got_ref, out_ref, held, leaving):
    part = out_ref.shape[4]
    copies = []
    for p in range(3):
        at = slice(9 * p * part, 9 * (p + 1) * part)
        total = keep_ref[:, at] + got_ref[:, at].astype(F32)
        for q in range(3):
            for r in range(3):
                lane = (3 * q + r) * part
                held[p, q, r] = total[:, lane : lane + part]
        copies.append(pltpu.make_async_copy(held.at[p], out_ref.at[p], leaving.at[p]))
        copies[-1].start()
    for copy in copies:
        copy.wait()


def sum_kernel(*refs):
    inputs, out_ref = refs[:-1], refs[-1]
    total = inputs[0][...]
    for ref in inputs[1:]:
        total = total + ref[...].astype(F32)
    out_ref[...] = total.astype(BF16)


def call(kernel, outs, scratch, inputs, placed=True, far=0):
    spaces = [pltpu.VMEM] * (len(inputs) - far) + [pltpu.HBM] * far
    return pl.pallas_call(
        kernel,
        out_shape=[pltpu.VMEM(v.shape, v.dtype) if placed else v for v in outs],
        in_specs=[pl.BlockSpec(memory_space=space) for space in spaces],
        out_specs=[pl.BlockSpec(memory_space=pltpu.VMEM)] * len(outs),
        scratch_shapes=scratch,
        compiler_params=pltpu.CompilerParams(vmem_limit_bytes=LIMIT),
    )(*[pltpu.with_memory_space_constraint(v, space) for v, space in zip(inputs, spaces)])


def fetch(weights, shapes):
    count = len(weights)
    return pl.pallas_call(
        fetch_kernel,
        out_shape=[pltpu.VMEM(shape, BF16) for shape in shapes],
        in_specs=[pl.BlockSpec(memory_space=pltpu.HBM)] * count,
        out_specs=[pl.BlockSpec(memory_space=pltpu.VMEM)] * count,
        scratch_shapes=[pltpu.SemaphoreType.DMA((count,))],
        compiler_params=pltpu.CompilerParams(vmem_limit_bytes=LIMIT),
    )(*[pltpu.with_memory_space_constraint(v, pltpu.HBM) for v in weights])


def gather(value):
    held = {0: value}
    k = lax.axis_size("chan") // 2
    while k:
        for j in list(held):
            held[j ^ k] = swap(held[j], "chan", k)
        k //= 2
    return [held[j] for j in sorted(held)]


def work(grad_out, feat_full, filters_full, upsample_weight, filters_half):
    n, m = lax.axis_size("chan"), lax.axis_size("grp")
    nx, ny, nz, ch = grad_out.shape
    half_x, half_y, half_z = nx // 2, n * ny // 2, nz // 2
    width = filters_half.shape[4]
    lanes = 27 * (ch // n)
    shape = jax.ShapeDtypeStruct
    edge = shape((HALO + 1, ny, nz, ch), BF16)
    own, first, last = call(
        load_kernel,
        [shape((2 * nx, ny, nz, ch), BF16), edge, edge],
        [pltpu.SemaphoreType.DMA((6,))],
        (grad_out, feat_full),
        far=2,
    )
    from_left = shift(last, "grp", 1)
    from_right = shift(first, "grp", -1)
    bricks = gather(own)
    (rim,) = call(
        lambda *refs: rims_kernel(m, *refs),
        [shape((2 * HALO + 2, ny, nz, ch), BF16)],
        [],
        (from_left, from_right),
    )
    rims = gather(rim)
    up = upsample_weight.shape[:3] + (width, ch)
    full, up = fetch((filters_full, upsample_weight), (filters_full.shape, up))
    keep, send = call(
        lambda *refs: taps_kernel(n, m, *refs),
        [shape((ch // 2, lanes), F32), shape((ch // 2, lanes), BF16)],
        [pltpu.VMEM((nx, n * ny + 2, nz, ch), BF16), pltpu.VMEM((ch, lanes), F32)],
        tuple(bricks),
    )
    (outer,) = call(
        lambda *refs: outer_kernel(n, m, *refs),
        [shape((2, ch // 2, lanes // 3), F32)],
        [pltpu.VMEM((4, n * ny + 2, nz, ch), BF16)],
        (*bricks, *rims),
    )
    got = swap(send, "grp", 1)
    (inner,) = call(
        lambda *refs: inner_kernel(n, *refs),
        [shape((2, nx + 2, n * ny, half_z, ch), F32)],
        [
            pltpu.VMEM((nx * ny, nz, ch), F32),
            pltpu.VMEM((4, half_x, n * ny + 2, nz, ch), BF16),
        ],
        (*bricks, full),
    )
    chunk = (half_y // n, half_x, half_z, filters_half.shape[3])
    chunks = call(
        lambda *refs: main_kernel(n, m, *refs),
        [shape(chunk, F32)] + [shape(chunk, BF16)] * (n - 1),
        [
            pltpu.VMEM((2 * HALO * ny, nz, ch), F32),
            pltpu.VMEM((4, HALO, n * ny + 2, nz, ch), BF16),
            pltpu.VMEM((3, half_y + 2, half_x + 2, half_z, width), F32),
            pltpu.VMEM((n,) + chunk, F32),
            pltpu.VMEM(filters_half.shape, BF16),
            pltpu.SemaphoreType.DMA((3,)),
        ],
        (*rims, inner, full, up, filters_half),
        far=1,
    )
    parts = [chunks[0]]
    for k in range(1, n):
        parts.append(swap(chunks[k], "chan", k))
    (grad_half,) = call(sum_kernel, [shape(chunk, BF16)], [], parts, False)
    for bit in range(1, m.bit_length() - 1):
        rows = keep.shape[0] // 2
        keep, send = call(
            lambda *refs: fold_kernel(bit, *refs),
            [shape((rows, lanes), F32), shape((rows, lanes), BF16)],
            [],
            (keep, got) if bit > 1 else (keep, got, outer),
        )
        got = swap(send, "grp", 2**bit)
    final = (3, 3, 3, ch // m, ch // n)
    taps_grad = pl.pallas_call(
        finish_kernel,
        out_shape=shape(final, F32),
        in_specs=[pl.BlockSpec(memory_space=pltpu.VMEM)] * 2,
        out_specs=pl.BlockSpec(memory_space=pltpu.HBM),
        scratch_shapes=[pltpu.VMEM(final, F32), pltpu.SemaphoreType.DMA((3,))],
        compiler_params=pltpu.CompilerParams(vmem_limit_bytes=LIMIT),
    )(*[pltpu.with_memory_space_constraint(v, pltpu.VMEM) for v in (keep, got)])
    return (grad_half, taps_grad)


def solution(mesh):
    in_specs = (
        P("grp", "chan", None, None),
        P("grp", "chan", None, None),
        P(),
        P(),
        P(None, None, None, None, "chan"),
    )
    out_specs = (P("chan", "grp", None, None), P(None, None, None, "grp", "chan"))
    return jax.shard_map(work, mesh=mesh, in_specs=in_specs, out_specs=out_specs, check_vma=False)
```
